32 devices in a mesh: fsdp: 8 (over y, x, core), tensor: 4 (over z).
Axes of the slice: x: 2, y: 2, z: 4, core: 2. Of those that a mesh axis runs over, the one named last changes fastest.
Arguments:
- tokens: bfloat16 [8192, 4096], P('fsdp'), may hold values from -6 to 6
- input_source: float32 [256, 16, 4096], P('tensor', None, 'fsdp'), may hold values from -0.09375 to 0.09375
- branch_source: float32 [256, 16, 4096], P('tensor', None, 'fsdp'), may hold values from -0.09375 to 0.09375
- output_source: float32 [256, 16, 4096], P('tensor', None, 'fsdp'), may hold values from -0.09375 to 0.09375
- gates_source: float32 [2, 16, 256, 256], P(None, None, 'fsdp', 'tensor'), may hold values from -0.375 to 0.375
- decay_param: float32 [16, 256], replicated, may hold values from -9 to 1
- block_order: int32 [16], replicated, may hold values from 0 to 15, each once
Outputs:
- mixed: bfloat16 [8192, 4096], P('fsdp', 'tensor')
- input_serve: bfloat16 [4096, 4096], P(None, 'tensor')
- branch_serve: bfloat16 [4096, 4096], P(None, 'tensor')
- output_serve: bfloat16 [4096, 4096], P(None, 'tensor')
- gates_serve: bfloat16 [2, 16, 256, 256], P(None, 'tensor')
The draws below stay inside these ranges and needn't reach their ends.
Inputs may be any that keep to these rules, and one draw needn't show every extreme that they name: `block_order`: every gate block appears exactly once.
All inputs are finite; a program needn't handle non-finite values.
Results may differ from the reference program's by a relative error of at most 0.013.
Values may be sent and summed in bfloat16 or wider, within the bound.
A program may use at most 128 MiB of HBM per device.

```python
import jax
import jax.numpy as jnp
from jax import lax

D = 4096
BLOCKS = 16
CHAN = 256
W = 4096
LEN = 256
TOK_DEV = 1024
TOKENS = 8192
N_TENSOR = 4


def shard_levels(rng, shape, cuts, least, largest):
    gain, own = 1.0, jax.random.fold_in(rng, 6)
    for dim, parts in cuts:
        steps = jnp.exp(jax.random.uniform(jax.random.fold_in(own, dim), (parts,), jnp.float32, least / len(cuts), largest / len(cuts)))
        gain = gain * jnp.repeat(steps, shape[dim] // parts).reshape([-1 if axis == dim else 1 for axis in range(len(shape))])
    return gain


def bell_draw(own_key, shape, scale, bound, cuts=(), held_as=jnp.bfloat16):
    level = shard_levels(own_key, shape, cuts, -0.22, 0.18) if cuts else 1.0
    entries = jax.random.normal(own_key, shape, jnp.float32) * scale * level
    return jnp.minimum(jnp.maximum(entries, -bound), bound).astype(held_as)


def setup_inputs(seed: int = 0) -> dict:
    key_of = jax.random.split(jax.random.key(seed), 8)
    tokens = bell_draw(key_of[0], (TOKENS, D), 1.0, 6.0, ((0, 8),))
    input_source = bell_draw(key_of[1], (CHAN, BLOCKS, D), D ** -0.5, 0.09375, ((0, 4), (2, 8)), jnp.float32)
    branch_source = bell_draw(key_of[2], (CHAN, BLOCKS, D), D ** -0.5, 0.09375, ((0, 4), (2, 8)), jnp.float32)
    output_source = bell_draw(key_of[3], (CHAN, BLOCKS, D), W ** -0.5, 0.09375, ((0, 4), (2, 8)), jnp.float32)
    gates_source = bell_draw(key_of[4], (2, BLOCKS, CHAN, CHAN), CHAN ** -0.5, 0.375, ((2, 8), (3, 4)), jnp.float32)
    decay_param = jnp.clip(jax.random.uniform(key_of[5], (BLOCKS, CHAN), jnp.float32, -9.0, 1.0), -9.0, 1.0)
    block_order = jax.random.permutation(key_of[6], BLOCKS).astype(jnp.int32)
    return {"tokens": tokens, "input_source": input_source, "branch_source": branch_source, "output_source": output_source, "gates_source": gates_source, "decay_param": decay_param, "block_order": block_order}


def serving_matrix(source, block_order):
    picked = jnp.take(source, block_order, axis=1)
    return jnp.transpose(picked, (2, 1, 0)).reshape(D, BLOCKS * CHAN).astype(jnp.bfloat16)

def combine_steps(earlier, latter):
    return (earlier[0] * latter[0], latter[0] * earlier[1] + latter[1])

def recurrence(features, input_serve, branch_serve, gates_serve, decay_rows):
    row_count = features.shape[0]
    branch_in = jnp.dot(features, input_serve, preferred_element_type=jnp.float32).astype(jnp.bfloat16)
    gate_pre = jnp.dot(features, branch_serve, preferred_element_type=jnp.float32)
    branch_wide = branch_in.astype(jnp.float32)
    blocked = branch_wide.reshape(row_count, BLOCKS, CHAN)
    gate_table = gates_serve.astype(jnp.float32)
    recur_pre = jnp.einsum('tbi,boi->tbo', blocked, gate_table[0]).reshape(row_count, -1)
    input_pre = jnp.einsum('tbi,boi->tbo', blocked, gate_table[1]).reshape(row_count, -1)
    recur_gate = jax.nn.sigmoid(recur_pre)
    input_gate = jax.nn.sigmoid(input_pre)
    log_decay = -8.0 * jax.nn.softplus(decay_rows) * recur_gate
    decay_step = jnp.exp(log_decay)
    drive_term = jnp.sqrt(1.0 - jnp.exp(2.0 * log_decay)) * (input_gate * branch_wide)
    replicas = row_count // TOK_DEV
    prompts = TOK_DEV // LEN
    shaped = (decay_step.reshape(replicas, LEN, prompts, -1), drive_term.reshape(replicas, LEN, prompts, -1))
    _, states = lax.associative_scan(combine_steps, shaped, axis=1)
    states = states.reshape(row_count, -1)
    return (states * jax.nn.gelu(gate_pre, approximate=True)).astype(jnp.bfloat16)

def reference(tokens, input_source, branch_source, output_source, gates_source, decay_param, block_order):
    input_serve = serving_matrix(input_source, block_order)
    branch_serve = serving_matrix(branch_source, block_order)
    output_serve = serving_matrix(output_source, block_order)
    gates_serve = jnp.transpose(jnp.take(gates_source, block_order, axis=1), (0, 1, 3, 2)).astype(jnp.bfloat16)
    decay_rows = jnp.take(decay_param, block_order, axis=0).reshape(BLOCKS * CHAN)
    gated = recurrence(tokens, input_serve, branch_serve, gates_serve, decay_rows)
    col_width = BLOCKS * CHAN // N_TENSOR
    running = jnp.zeros((tokens.shape[0], D), jnp.float32)
    for tp_group in range(N_TENSOR):
        lower = tp_group * col_width
        partial_value = jnp.dot(gated[:, lower:lower + col_width], output_serve[:, lower:lower + col_width].T, preferred_element_type=jnp.float32)
        rounded = lax.optimization_barrier(partial_value.astype(jnp.bfloat16))
        running = running + rounded.astype(jnp.float32)
    return (running.astype(jnp.bfloat16), input_serve, branch_serve, output_serve, gates_serve)
```

```python
import functools
import jax
import jax.numpy as jnp
from jax import lax
from jax.experimental import pallas as pl
from jax.experimental.pallas import tpu as pltpu
from jax.sharding import PartitionSpec as P

LEN = 256
SUB = 8
VMEM_LIMIT = 60 * 2**20
MESH = pl.DeviceIdType.MESH
NT = (((1,), (1,)), ((), ()))


def recur_body(
    prompts, x_ref, pre_ref, g_ref, r_ref, wi_ref, wb_ref,
    o_ref, wi_out, wb_out, g_out, a_s, d_s, carry,
):
    @pl.when(pl.program_id(1) == 0)
    def _():
        carry[...] = jnp.zeros_like(carry)
        g_out[...] = g_ref[...]

    wi_out[...] = wi_ref[...]
    wb_out[...] = wb_ref[...]
    x = x_ref[...]
    pre_r = lax.dot_general(x, g_ref[0, 0], NT, preferred_element_type=jnp.float32)
    pre_i = lax.dot_general(x, g_ref[1, 0], NT, preferred_element_type=jnp.float32)
    a = jnp.exp(r_ref[0] * jax.nn.sigmoid(pre_r))
    a_s[...] = a
    d_s[...] = jnp.sqrt(jnp.maximum(1.0 - a * a, 0.0)) * (
        jax.nn.sigmoid(pre_i) * x.astype(jnp.float32)
    )
    rows, chan = a_s.shape
    group = lax.broadcasted_iota(jnp.int32, (SUB, chan), 0) // prompts

    def last(v):
        res = v
        for g in range(SUB // prompts - 1):
            res = jnp.where(group == g, pltpu.roll(v, (g + 1) * prompts, 0), res)
        return res

    def step(i, c):
        at = pl.ds(pl.multiple_of(i * SUB, SUB), SUB)
        a = a_s[at, :]
        d = d_s[at, :]
        shift = 1
        while shift < SUB // prompts:
            a_sh = pltpu.roll(a, shift * prompts, 0)
            d_sh = pltpu.roll(d, shift * prompts, 0)
            d = jnp.where(group >= shift, a * d_sh + d, d)
            a = jnp.where(group >= shift, a * a_sh, a)
            shift *= 2
        d_s[at, :] = a * c + d
        return last(a) * c + last(d)

    carry[...] = lax.fori_loop(0, rows // SUB, step, carry[...], unroll=8)
    o_ref[...] = (d_s[...] * jax.nn.gelu(pre_ref[...], approximate=True)).astype(o_ref.dtype)


def recur(branch_in, gate_pre, gates, rate, wi, wb, prompts):
    rows, width = branch_in.shape
    blocks, chan = gates.shape[1], gates.shape[2]
    tile = min(rows, 256)
    tiles = rows // tile
    part = wi.shape[0] // (blocks * tiles)
    cell = pl.BlockSpec((tile, chan), lambda b, t: (t, b))
    gate = pl.BlockSpec((2, 1, chan, chan), lambda b, t: (0, b, 0, 0))
    slab = pl.BlockSpec((part, width), lambda b, t: (b * tiles + t, 0))
    return pl.pallas_call(
        functools.partial(recur_body, prompts),
        grid=(blocks, tiles),
        in_specs=[cell, cell, gate, pl.BlockSpec((1, 1, chan), lambda b, t: (b, 0, 0)), slab, slab],
        out_specs=[cell, slab, slab, gate],
        out_shape=[
            jax.ShapeDtypeStruct((rows, width), jnp.bfloat16),
            jax.ShapeDtypeStruct(wi.shape, wi.dtype),
            jax.ShapeDtypeStruct(wb.shape, wb.dtype),
            jax.ShapeDtypeStruct(gates.shape, gates.dtype),
        ],
        scratch_shapes=[
            pltpu.VMEM((tile, chan), jnp.float32),
            pltpu.VMEM((tile, chan), jnp.float32),
            pltpu.VMEM((SUB, chan), jnp.float32),
        ],
        compiler_params=pltpu.CompilerParams(
            dimension_semantics=("arbitrary", "arbitrary"), vmem_limit_bytes=VMEM_LIMIT
        ),
        cost_estimate=pl.CostEstimate(
            flops=4 * rows * width * chan, bytes_accessed=8 * rows * width, transcendentals=6 * rows * width
        ),
        name="recur",
    )(branch_in, gate_pre, gates, rate, wi, wb)


def places():
    f = lax.axis_index("fsdp")
    sib = f + 1 - 2 * (f % 2)
    xp = f + 2 - 4 * ((f // 2) % 2)
    yp = f + 4 - 8 * (f // 4)
    diag = xp + 4 - 8 * (xp // 4)
    return f, sib, xp, yp, diag


def greet(zs, z, peers):
    barrier = pltpu.get_barrier_semaphore()
    for peer in peers:
        pl.semaphore_signal(barrier, inc=1, device_id={"fsdp": peer}, device_id_type=MESH)
    for k in range(1, zs):
        pl.semaphore_signal(
            barrier, inc=1, device_id={"tensor": (z + k) % zs}, device_id_type=MESH
        )
    pl.semaphore_wait(barrier, len(peers) + zs - 1)


def gatherer(view, f_send, f_recv):
    f, sib, xp, yp, diag = places()
    sent = {}

    def send(q, i, owner, peer):
        at = view(q, owner)
        sent[q, i] = pltpu.make_async_remote_copy(
            src_ref=at,
            dst_ref=at,
            send_sem=f_send.at[q, i],
            recv_sem=f_recv.at[q, i],
            device_id={"fsdp": peer},
            device_id_type=MESH,
        )
        sent[q, i].start()

    def first(q):
        for i, peer in enumerate((xp, yp, sib)):
            send(q, i, f, peer)

    def relay(q):
        sent[q, 0].wait_recv()
        if q % 2 == 0:
            send(q, 3, xp, yp)
        send(q, 4, xp, sib)
        sent[q, 1].wait_recv()
        if q % 2 == 1:
            send(q, 3, yp, xp)
        send(q, 5, yp, sib)

    def across(q):
        sent[q, 3].wait_recv()
        send(q, 6, diag, sib)

    def have(q, i):
        sent[q, i].wait_recv()

    def drain(qs):
        for q in qs:
            for i in range(7):
                sent[q, i].wait_send()

    return first, relay, across, have, drain


def spread_body(
    order, src0, src1, src2, perm, gsrc, tokens,
    out0, out1, piece2, gates_out, x_out, pre_out,
    xb, sbuf, gsend, held, gheld, gfull, wfull, tok, acc,
    tok_sem, own_sem, z_send, z_recv, put_sem, f_send, f_recv,
):
    srcs = (src0, src1, src2)
    z = lax.axis_index("tensor")
    f, sib, xp, yp, diag = places()
    zs, per, chan = held.shape[1], held.shape[2], held.shape[3]
    rows = held.shape[4]
    half = rows // 2
    ghalf = gheld.shape[3] // 2
    group = per * chan
    tok_copy = pltpu.make_async_copy(tokens, tok, tok_sem)
    tok_copy.start()

    def cast(w):
        xb[...] = srcs[w][...].reshape(xb.shape).astype(jnp.bfloat16)
        for k in range(zs):
            part = jnp.dot(
                perm[k * group : (k + 1) * group, :], xb[...], preferred_element_type=jnp.float32
            )
            sbuf[w, k * per : (k + 1) * per] = part.astype(jnp.bfloat16).reshape(per, chan, rows)

    cast(0)
    greet(zs, z, (sib, xp, yp))

    def z_source(q, to):
        if q == 6:
            return gsend.at[:, pl.ds(to * per, per)]
        return sbuf.at[q // 2, pl.ds(to * per, per), :, pl.ds((q % 2) * half, half)]

    def z_target(q):
        if q == 6:
            return gheld.at[z]
        return held.at[q // 2, z, :, :, pl.ds((q % 2) * half, half)]

    a2a, own = {}, {}
    queue = [0, 1, 2, 6, 3, 4, 5]

    def depart():
        q = queue.pop(0)
        for k in range(1, zs):
            to = (z + k) % zs
            a2a[q, k] = pltpu.make_async_remote_copy(
                src_ref=z_source(q, to),
                dst_ref=z_target(q),
                send_sem=z_send.at[q, k],
                recv_sem=z_recv.at[q, k],
                device_id={"tensor": to},
                device_id_type=MESH,
            )
            a2a[q, k].start()
        own[q] = pltpu.make_async_copy(z_source(q, z), z_target(q), own_sem.at[q])
        own[q].start()

    depart()
    depart()
    cast(1)
    cast(2)
    for g in range(gsend.shape[0]):
        for j in range(gsend.shape[1]):
            gsend[g, j] = gsrc[g, order[j]].astype(jnp.bfloat16)

    def arrive(q):
        own[q].wait()
        for k in range(1, zs):
            a2a[q, k].wait_recv()
        if queue:
            depart()

    def slab(q, b):
        at = slice((q % 2) * half, (q % 2) * half + half)
        return jnp.concatenate([held[q // 2, s, b, :, at] for s in range(zs)], axis=0).T

    def view(q, owner):
        if q >= 4:
            return gfull.at[:, :, pl.ds(owner * 2 * ghalf + (q - 4) * ghalf, ghalf)]
        return wfull.at[q // 2, pl.ds(owner * rows + (q % 2) * half, half)]

    send_first, relay, across, have, drain = gatherer(view, f_send, f_recv)

    def first(q):
        if q < 4:
            arrive(q)
            at = pl.ds(pl.multiple_of(f * rows + (q % 2) * half, half), half)
            for b in range(per):
                width = chan * zs
                wfull[q // 2, at, b * width : (b + 1) * width] = slab(q, b)
        send_first(q)

    def first_out(q):
        arrive(q)
        at = slice((q % 2) * half, (q % 2) * half + half)
        for b in range(per):
            width = chan * zs
            piece2[at, b * width : (b + 1) * width] = slab(q, b)

    put = []
    tile = 256
    deep = 2 * rows
    tiles = tok.shape[0] // tile

    def product(w, part, mode):
        base = pl.multiple_of(part * deep, deep)
        outs = (out0, out1)
        copy = pltpu.make_async_copy(
            wfull.at[w, pl.ds(base, deep)], outs[w].at[pl.ds(base, deep)], put_sem.at[len(put)]
        )
        copy.start()
        put.append(copy)
        dst = (acc, pre_out)[w]

        def step(i, c):
            at = pl.ds(pl.multiple_of(i * tile, tile), tile)
            value = jnp.dot(
                tok[at, pl.ds(base, deep)],
                wfull[w, pl.ds(base, deep), :],
                preferred_element_type=jnp.float32,
            )
            if mode != "first":
                value = value + dst[at, :]
            if w == 0 and mode == "last":
                x_out[at, :] = value.astype(jnp.bfloat16)
            else:
                dst[at, :] = value
            return c

        lax.fori_loop(0, tiles, step, 0)

    chip, chip_x, chip_y, chip_d = f // 2, xp // 2, yp // 2, diag // 2

    first(0)
    first(1)
    relay(0)
    first(2)
    arrive(6)
    for h in range(2):
        for g in range(gfull.shape[0]):
            for b in range(per):
                at = pl.ds(pl.multiple_of((f * 2 + h) * ghalf, ghalf), ghalf)
                gfull[g, b, at, :] = jnp.concatenate(
                    [gheld[s, g, b, h * ghalf : (h + 1) * ghalf, :] for s in range(zs)], axis=1
                )
    first(4)
    first(5)
    relay(1)
    first(3)
    tok_copy.wait()
    have(0, 2)
    have(1, 2)
    product(0, chip, "first")
    across(0)
    relay(2)
    have(0, 4)
    have(1, 4)
    product(0, chip_x, "more")
    relay(4)
    relay(5)
    first_out(4)
    across(1)
    have(0, 5)
    have(1, 5)
    product(0, chip_y, "more")
    relay(3)
    have(0, 6)
    have(1, 6)
    product(0, chip_d, "last")
    first_out(5)
    for q in (4, 5, 2):
        across(q)
    have(2, 2)
    have(3, 2)
    product(1, chip, "first")
    have(2, 4)
    have(3, 4)
    product(1, chip_x, "more")
    across(3)
    have(2, 5)
    have(3, 5)
    product(1, chip_y, "more")
    for q in (4, 5):
        for i in (2, 4, 5, 6):
            have(q, i)
    for g in range(gfull.shape[0]):
        for b in range(per):
            gates_out[g, b] = gfull[g, b].T
    have(2, 6)
    have(3, 6)
    product(1, chip_d, "last")
    for copy in put:
        copy.wait()
    drain(range(6))
    for q in range(7):
        for k in range(1, zs):
            a2a[q, k].wait_send()


def spread(order, sources, gates, tokens, zs, fs):
    chan, blocks, rows = sources[0].shape
    kinds, _, gin, gout = gates.shape
    per = blocks // zs
    width = per * chan * zs
    toks = tokens.shape[0]
    perm = (
        (order[:, None, None, None] == jnp.arange(blocks)[None, None, None, :])
        & (jnp.arange(chan)[None, :, None, None] == jnp.arange(chan)[None, None, :, None])
    ).astype(jnp.bfloat16).reshape(blocks * chan, chan * blocks)
    full = jax.ShapeDtypeStruct((rows * fs, width), jnp.bfloat16)
    vmem = pl.BlockSpec(memory_space=pltpu.VMEM)
    hbm = pl.BlockSpec(memory_space=pl.ANY)
    dma = pltpu.SemaphoreType.DMA
    return pl.pallas_call(
        spread_body,
        in_specs=[pl.BlockSpec(memory_space=pltpu.SMEM)] + [vmem] * 5 + [hbm],
        out_specs=[hbm, hbm, vmem, vmem, vmem, vmem],
        out_shape=[
            full,
            full,
            jax.ShapeDtypeStruct((rows, width), jnp.bfloat16),
            jax.ShapeDtypeStruct((kinds, per, gout * zs, gin * fs), jnp.bfloat16),
            jax.ShapeDtypeStruct((toks, width), jnp.bfloat16),
            jax.ShapeDtypeStruct((toks, width), jnp.float32),
        ],
        scratch_shapes=[
            pltpu.VMEM((chan * blocks, rows), jnp.bfloat16),
            pltpu.VMEM((3, blocks, chan, rows), jnp.bfloat16),
            pltpu.VMEM((kinds, blocks, gin, gout), jnp.bfloat16),
            pltpu.VMEM((3, zs, per, chan, rows), jnp.bfloat16),
            pltpu.VMEM((zs, kinds, per, gin, gout), jnp.bfloat16),
            pltpu.VMEM((kinds, per, gin * fs, gout * zs), jnp.bfloat16),
            pltpu.VMEM((2, rows * fs, width), jnp.bfloat16),
            pltpu.VMEM(tokens.shape, jnp.bfloat16),
            pltpu.VMEM((toks, width), jnp.float32),
            dma,
            dma((7,)),
            dma((7, zs)),
            dma((7, zs)),
            dma((8,)),
            dma((6, 7)),
            dma((6, 7)),
        ],
        compiler_params=pltpu.CompilerParams(
            collective_id=0, has_side_effects=True, vmem_limit_bytes=VMEM_LIMIT
        ),
        name="spread",
    )(order, *sources, perm, gates, tokens)


def chain_body(
    gated, piece, out, mixed, wfull, outgo, right_in, left_in, put_sem,
    r_send, r_recv, l_send, l_recv, f_send, f_recv,
):
    z = lax.axis_index("tensor")
    f, sib, xp, yp, diag = places()
    rows = piece.shape[0]
    parts = 4
    part = rows // parts
    zs = lax.axis_size("tensor")
    owners = wfull.shape[0] // rows
    cut = outgo.shape[3]
    rt = outgo.shape[2]
    halves = rows // cut
    wfull[pl.ds(pl.multiple_of(f * rows, rows), rows), :] = piece[...]

    greet(zs, z, (sib, xp, yp))

    def view(q, owner):
        return wfull.at[pl.ds(owner * rows + q * part, part)]

    send_first, relay, across, have, drain = gatherer(view, f_send, f_recv)

    cuts = owners * halves
    quarter = cuts // zs
    times = gated.shape[0] // rt
    right = [(d, t) for q in range(zs - 1, 0, -1) for d in ordered(q, quarter, halves) for t in range(times)]
    left = [(d, t) for q in range(zs - 1) for d in ordered(q, quarter, halves) for t in range(times)]

    def term(d, t):
        return lax.dot_general(
            gated[t * rt : (t + 1) * rt, :],
            wfull[pl.ds(d * cut, cut), :],
            NT,
            preferred_element_type=jnp.float32,
        )

    def copy(d, t, forward):
        ins = right_in if forward else left_in
        return pltpu.make_async_remote_copy(
            src_ref=outgo.at[d, t],
            dst_ref=ins.at[d, t],
            send_sem=(r_send if forward else l_send).at[d, t],
            recv_sem=(r_recv if forward else l_recv).at[d, t],
            device_id={"tensor": (z + (1 if forward else zs - 1)) % zs},
            device_id_type=MESH,
        )

    def head(d, t, forward):
        outgo[d, t] = term(d, t).astype(jnp.bfloat16)
        copy(d, t, forward).start()

    def pass_on(d, t, forward):
        value = term(d, t)
        copy(d, t, forward).wait_recv()
        ins = right_in if forward else left_in
        outgo[d, t] = (value + ins[d, t].astype(jnp.float32)).astype(jnp.bfloat16)
        copy(d, t, forward).start()

    def both(k):
        for forward, (d, t) in ((True, right[k]), (False, left[k])):
            q = d // quarter
            inner = [i for i in range(1, zs - 1) if (i < q if forward else i > q)]

            @pl.when(z == (0 if forward else zs - 1))
            def _():
                head(d, t, forward)

            if inner:
                @pl.when((z >= inner[0]) & (z <= inner[-1]))
                def _():
                    pass_on(d, t, forward)

    for q in range(parts):
        send_first(q)
    relay(0)
    relay(1)
    across(0)
    across(1)
    for q in (0, 1):
        for i in (2, 4, 5, 6):
            have(q, i)
    both(0)
    relay(2)
    both(1)
    relay(3)
    both(2)
    across(2)
    across(3)
    both(3)
    for q in (2, 3):
        for i in (2, 4, 5, 6):
            have(q, i)
    put = pltpu.make_async_copy(wfull, out, put_sem)
    put.start()
    for k in range(4, len(right)):
        both(k)

    for i, d0 in enumerate(ordered(0, quarter, halves)):
        for t in range(times):
            d = z * quarter + d0
            value = lax.dot_general(
                gated[t * rt : (t + 1) * rt, :],
                wfull[pl.ds(pl.multiple_of(d * cut, cut), cut), :],
                NT,
                preferred_element_type=jnp.float32,
            )
            at = (slice(t * rt, (t + 1) * rt), slice(d0 * cut, (d0 + 1) * cut))

            @pl.when(z == 0)
            def _():
                copy(d, t, False).wait_recv()
                mixed[at] = (value + left_in[d, t].astype(jnp.float32)).astype(mixed.dtype)

            @pl.when(z == zs - 1)
            def _():
                copy(d, t, True).wait_recv()
                mixed[at] = (value + right_in[d, t].astype(jnp.float32)).astype(mixed.dtype)

            @pl.when((z > 0) & (z < zs - 1))
            def _():
                copy(d, t, False).wait_recv()
                copy(d, t, True).wait_recv()
                mixed[at] = (
                    value + left_in[d, t].astype(jnp.float32) + right_in[d, t].astype(jnp.float32)
                ).astype(mixed.dtype)

    for d in range(cuts):
        for t in range(times):
            q = d // quarter
            if q > 0:
                @pl.when(z < q)
                def _():
                    copy(d, t, True).wait_send()
            if q < zs - 1:
                @pl.when(z > q)
                def _():
                    copy(d, t, False).wait_send()
    drain(range(parts))
    put.wait()


def ordered(q, quarter, halves):
    base = range(q * quarter, (q + 1) * quarter)
    return sorted(base, key=lambda d: (d % halves, d))


def chain(gated, piece, zs, fs):
    rows, width = piece.shape
    toks = gated.shape[0]
    depth = rows * fs
    cut, rt = rows // 2, toks // 2
    vmem = pl.BlockSpec(memory_space=pltpu.VMEM)
    dma = pltpu.SemaphoreType.DMA
    grid = (depth // cut, toks // rt)
    return pl.pallas_call(
        chain_body,
        in_specs=[vmem, vmem],
        out_specs=[pl.BlockSpec(memory_space=pl.ANY), vmem],
        out_shape=[
            jax.ShapeDtypeStruct((depth, width), jnp.bfloat16),
            jax.ShapeDtypeStruct((toks, depth // zs), jnp.bfloat16),
        ],
        scratch_shapes=[
            pltpu.VMEM((depth, width), jnp.bfloat16),
            pltpu.VMEM((*grid, rt, cut), jnp.bfloat16),
            pltpu.VMEM((*grid, rt, cut), jnp.bfloat16),
            pltpu.VMEM((*grid, rt, cut), jnp.bfloat16),
            dma,
            dma(grid),
            dma(grid),
            dma(grid),
            dma(grid),
            dma((4, 7)),
            dma((4, 7)),
        ],
        compiler_params=pltpu.CompilerParams(
            collective_id=1, has_side_effects=True, vmem_limit_bytes=VMEM_LIMIT
        ),
        name="chain",
    )(gated, piece)


def dup_body(x_ref, y_ref, x_out, y_out):
    x_out[...] = x_ref[...]
    y_out[...] = y_ref[...]


def dup(x, y):
    steps = 8
    specs = [pl.BlockSpec((a.shape[0] // steps, a.shape[1]), lambda i: (i, 0)) for a in (x, y)]
    return pl.pallas_call(
        dup_body,
        grid=(steps,),
        in_specs=specs,
        out_specs=specs,
        out_shape=[jax.ShapeDtypeStruct(a.shape, a.dtype) for a in (x, y)],
        cost_estimate=pl.CostEstimate(flops=0, bytes_accessed=4 * (x.size + y.size), transcendentals=0),
        name="dup",
    )(x, y)


def on_device(
    tokens, input_source, branch_source, output_source, gates_source, decay_param, block_order
):
    zs, fs = lax.axis_size("tensor"), lax.axis_size("fsdp")
    blocks = block_order.shape[0]
    per_dev = blocks // zs
    prompts = tokens.shape[0] // LEN
    picked = (block_order[:, None] == jnp.arange(blocks)[None, :]).astype(jnp.float32)
    soft = -8.0 * jax.nn.softplus(decay_param)
    own = lax.dynamic_slice_in_dim(picked, lax.axis_index("tensor") * per_dev, per_dev)
    rate = jnp.sum(own[:, :, None] * soft[None, :, :], axis=1)[:, None, :]
    sources = (input_source, branch_source, output_source)
    if fs == 8 and zs == 4:
        wi, wb, piece, gates, branch_in, gate_pre = spread(
            block_order, sources, gates_source, tokens, zs, fs
        )
        gated, wi, wb, gates = recur(branch_in, gate_pre, gates, rate, wi, wb, prompts)
        wo, mixed = chain(gated, piece, zs, fs)
        wo, mixed = dup(wo, mixed)
        return mixed, wi, wb, wo, gates
    hot = picked.astype(jnp.bfloat16)
    sectioned = tuple(
        jnp.einsum(
            "jb,cbr->cjr", hot, s.astype(jnp.bfloat16), preferred_element_type=jnp.float32
        ).astype(jnp.bfloat16)
        for s in sources
    )
    gate_sectioned = jnp.einsum(
        "jb,gbio->gjio", hot, gates_source.astype(jnp.bfloat16), preferred_element_type=jnp.float32
    ).astype(jnp.bfloat16)
    gate_group = lax.all_to_all(gate_sectioned, "tensor", split_axis=1, concat_axis=3, tiled=True)
    gates = lax.all_gather(jnp.transpose(gate_group, (0, 1, 3, 2)), "fsdp", axis=3, tiled=True)
    regrouped = lax.all_to_all(sectioned, "tensor", split_axis=1, concat_axis=0, tiled=True)
    wi, wb, wo = (
        lax.all_gather(
            jnp.transpose(w, (2, 1, 0)).reshape(w.shape[2], -1), "fsdp", axis=0, tiled=True
        )
        for w in regrouped
    )
    branch_in = jnp.dot(tokens, wi, preferred_element_type=jnp.float32).astype(jnp.bfloat16)
    gate_pre = jnp.dot(tokens, wb, preferred_element_type=jnp.float32)
    gated, wi, wb, gates = recur(branch_in, gate_pre, gates, rate, wi, wb, prompts)
    partial_value = lax.dot_general(gated, wo, NT, preferred_element_type=jnp.float32)
    mixed = lax.psum_scatter(
        partial_value.astype(jnp.bfloat16), "tensor", scatter_dimension=1, tiled=True
    )
    return mixed, wi, wb, wo, gates


def solution(mesh):
    return jax.shard_map(
        on_device,
        mesh=mesh,
        in_specs=(
            P("fsdp", None),
            P("tensor", None, "fsdp"),
            P("tensor", None, "fsdp"),
            P("tensor", None, "fsdp"),
            P(None, None, "fsdp", "tensor"),
            P(),
            P(),
        ),
        out_specs=(
            P("fsdp", "tensor"),
            P(None, "tensor"),
            P(None, "tensor"),
            P(None, "tensor"),
            P(None, "tensor", None, None),
        ),
        check_vma=False,
    )
```

```python
import functools
import jax
import jax.numpy as jnp
from jax import lax
from jax.experimental import pallas as pl
from jax.experimental.pallas import tpu as pltpu
from jax.sharding import PartitionSpec as P

LEN = 256
SUB = 8
VMEM_LIMIT = 60 * 2**20
MESH = pl.DeviceIdType.MESH
NT = (((1,), (1,)), ((), ()))


def recur_body(
    prompts, x_ref, pre_ref, g_ref, r_ref, wi_ref, wb_ref,
    o_ref, wi_out, wb_out, g_out, a_s, d_s, carry,
):
    @pl.when(pl.program_id(1) == 0)
    def _():
        carry[...] = jnp.zeros_like(carry)
        g_out[...] = g_ref[...]

    wi_out[...] = wi_ref[...]
    wb_out[...] = wb_ref[...]
    x = x_ref[...]
    pre_r = lax.dot_general(x, g_ref[0, 0], NT, preferred_element_type=jnp.float32)
    pre_i = lax.dot_general(x, g_ref[1, 0], NT, preferred_element_type=jnp.float32)
    a = jnp.exp(r_ref[0] * jax.nn.sigmoid(pre_r))
    a_s[...] = a
    d_s[...] = jnp.sqrt(jnp.maximum(1.0 - a * a, 0.0)) * (
        jax.nn.sigmoid(pre_i) * x.astype(jnp.float32)
    )
    rows, chan = a_s.shape
    group = lax.broadcasted_iota(jnp.int32, (SUB, chan), 0) // prompts

    def last(v):
        res = v
        for g in range(SUB // prompts - 1):
            res = jnp.where(group == g, pltpu.roll(v, (g + 1) * prompts, 0), res)
        return res

    def step(i, c):
        at = pl.ds(pl.multiple_of(i * SUB, SUB), SUB)
        a = a_s[at, :]
        d = d_s[at, :]
        shift = 1
        while shift < SUB // prompts:
            a_sh = pltpu.roll(a, shift * prompts, 0)
            d_sh = pltpu.roll(d, shift * prompts, 0)
            d = jnp.where(group >= shift, a * d_sh + d, d)
            a = jnp.where(group >= shift, a * a_sh, a)
            shift *= 2
        d_s[at, :] = a * c + d
        return last(a) * c + last(d)

    carry[...] = lax.fori_loop(0, rows // SUB, step, carry[...], unroll=8)
    o_ref[...] = (d_s[...] * jax.nn.gelu(pre_ref[...], approximate=True)).astype(o_ref.dtype)


def recur(branch_in, gate_pre, gates, rate, wi, wb, prompts):
    rows, width = branch_in.shape
    blocks, chan = gates.shape[1], gates.shape[2]
    tile = min(rows, 256)
    tiles = rows // tile
    part = wi.shape[0] // (blocks * tiles)
    cell = pl.BlockSpec((tile, chan), lambda b, t: (t, b))
    gate = pl.BlockSpec((2, 1, chan, chan), lambda b, t: (0, b, 0, 0))
    slab = pl.BlockSpec((part, width), lambda b, t: (b * tiles + t, 0))
    return pl.pallas_call(
        functools.partial(recur_body, prompts),
        grid=(blocks, tiles),
        in_specs=[cell, cell, gate, pl.BlockSpec((1, 1, chan), lambda b, t: (b, 0, 0)), slab, slab],
        out_specs=[cell, slab, slab, gate],
        out_shape=[
            jax.ShapeDtypeStruct((rows, width), jnp.bfloat16),
            jax.ShapeDtypeStruct(wi.shape, wi.dtype),
            jax.ShapeDtypeStruct(wb.shape, wb.dtype),
            jax.ShapeDtypeStruct(gates.shape, gates.dtype),
        ],
        scratch_shapes=[
            pltpu.VMEM((tile, chan), jnp.float32),
            pltpu.VMEM((tile, chan), jnp.float32),
            pltpu.VMEM((SUB, chan), jnp.float32),
        ],
        compiler_params=pltpu.CompilerParams(
            dimension_semantics=("arbitrary", "arbitrary"), vmem_limit_bytes=VMEM_LIMIT
        ),
        cost_estimate=pl.CostEstimate(
            flops=4 * rows * width * chan, bytes_accessed=8 * rows * width, transcendentals=6 * rows * width
        ),
        name="recur",
    )(branch_in, gate_pre, gates, rate, wi, wb)


def places():
    f = lax.axis_index("fsdp")
    sib = f + 1 - 2 * (f % 2)
    xp = f + 2 - 4 * ((f // 2) % 2)
    yp = f + 4 - 8 * (f // 4)
    diag = xp + 4 - 8 * (xp // 4)
    return f, sib, xp, yp, diag


def greet(zs, z, peers):
    barrier = pltpu.get_barrier_semaphore()
    for peer in peers:
        pl.semaphore_signal(barrier, inc=1, device_id={"fsdp": peer}, device_id_type=MESH)
    for k in range(1, zs):
        pl.semaphore_signal(
            barrier, inc=1, device_id={"tensor": (z + k) % zs}, device_id_type=MESH
        )
    pl.semaphore_wait(barrier, len(peers) + zs - 1)


def gatherer(view, f_send, f_recv):
    f, sib, xp, yp, diag = places()

    def make(q, i):
        near, far = ((xp, yp), (yp, xp))[q % 2]
        owner, peer = (
            (f, xp), (f, yp), (f, sib), (near, far), (xp, sib), (yp, sib), (diag, sib),
        )[i]
        at = view(q, owner)
        return pltpu.make_async_remote_copy(
            src_ref=at,
            dst_ref=at,
            send_sem=f_send.at[q, i],
            recv_sem=f_recv.at[q, i],
            device_id={"fsdp": peer},
            device_id_type=MESH,
        )

    def first(q):
        for i in range(3):
            make(q, i).start()

    def relay(q):
        make(q, 0).wait_recv()
        if q % 2 == 0:
            make(q, 3).start()
        make(q, 4).start()
        make(q, 1).wait_recv()
        if q % 2 == 1:
            make(q, 3).start()
        make(q, 5).start()

    def across(q):
        make(q, 3).wait_recv()
        make(q, 6).start()

    def have(q, *ways):
        for i in ways:
            make(q, i).wait_recv()

    def drain(qs):
        for q in qs:
            for i in range(7):
                make(q, i).wait_send()

    return first, relay, across, have, drain


def spread_body(
    order, src0, src1, src2, gsrc, tokens,
    out0, out1, piece2, extra, gates_out, x_out, pre_out,
    perm, xb, sbuf, gsend, held, gheld, gfull, wfull, tok, acc,
    tok_sem, own_sem, z_send, z_recv, e_send, e_recv, put_sem, f_send, f_recv,
):
    srcs = (src0, src1, src2)
    z = lax.axis_index("tensor")
    f, sib, xp, yp, diag = places()
    zs, per, chan = held.shape[1], held.shape[2], held.shape[3]
    rows = held.shape[4]
    half = rows // 2
    ghalf = gheld.shape[3] // 2
    group = per * chan
    tok_copy = pltpu.make_async_copy(tokens, tok, tok_sem)
    tok_copy.start()

    def cast(w):
        xb[...] = srcs[w][...].reshape(xb.shape).astype(jnp.bfloat16)
        for k in range(zs):
            part = jnp.dot(
                perm[k * group : (k + 1) * group, :], xb[...], preferred_element_type=jnp.float32
            )
            sbuf[w, k * per : (k + 1) * per] = part.astype(jnp.bfloat16).reshape(per, chan, rows)

    blocks = sbuf.shape[1]
    column = lax.broadcasted_iota(jnp.int32, (chan, perm.shape[1]), 1)
    channel = lax.broadcasted_iota(jnp.int32, (chan, perm.shape[1]), 0) * blocks
    for j in range(blocks):
        perm[j * chan : (j + 1) * chan, :] = jnp.where(
            column == channel + order[j], 1.0, 0.0
        ).astype(jnp.bfloat16)
    cast(0)
    greet(zs, z, (sib, xp, yp))

    def z_source(q, to):
        if q == 6:
            return gsend.at[:, pl.ds(to * per, per)]
        return sbuf.at[q // 2, pl.ds(to * per, per), :, pl.ds((q % 2) * half, half)]

    def z_target(q):
        if q == 6:
            return gheld.at[z]
        return held.at[q // 2, z, :, :, pl.ds((q % 2) * half, half)]

    a2a, own = {}, {}
    queue = [0, 1, 2, 6, 3, 4, 5]

    def depart():
        q = queue.pop(0)
        for k in range(1, zs):
            to = (z + k) % zs
            a2a[q, k] = pltpu.make_async_remote_copy(
                src_ref=z_source(q, to),
                dst_ref=z_target(q),
                send_sem=z_send.at[q, k],
                recv_sem=z_recv.at[q, k],
                device_id={"tensor": to},
                device_id_type=MESH,
            )
            a2a[q, k].start()
        own[q] = pltpu.make_async_copy(z_source(q, z), z_target(q), own_sem.at[q])
        own[q].start()

    depart()
    cast(1)
    cast(2)
    for g in range(gsend.shape[0]):
        for j in range(gsend.shape[1]):
            gsend[g, j] = gsrc[g, order[j]].astype(jnp.bfloat16)

    def arrive(q):
        own[q].wait()
        for k in range(1, zs):
            a2a[q, k].wait_recv()
        for _ in range(2 if q == 0 else 1):
            if queue:
                depart()

    def slab(q, b):
        at = slice((q % 2) * half, (q % 2) * half + half)
        return jnp.concatenate([held[q // 2, s, b, :, at] for s in range(zs)], axis=0).T

    def view(q, owner):
        if q >= 4:
            return gfull.at[:, :, pl.ds(owner * 2 * ghalf + (q - 4) * ghalf, ghalf)]
        return wfull.at[q // 2, pl.ds(owner * rows + (q % 2) * half, half)]

    send_first, relay, across, have, drain = gatherer(view, f_send, f_recv)

    def first(q):
        if q < 4:
            arrive(q)
            at = pl.ds(pl.multiple_of(f * rows + (q % 2) * half, half), half)
            for b in range(per):
                width = chan * zs
                wfull[q // 2, at, b * width : (b + 1) * width] = slab(q, b)
        send_first(q)

    def first_out(q):
        arrive(q)
        at = slice((q % 2) * half, (q % 2) * half + half)
        for b in range(per):
            width = chan * zs
            piece2[at, b * width : (b + 1) * width] = slab(q, b)
        for end, inner in ((0, 1), (zs - 1, zs - 2)):
            @pl.when(z == end)
            def _():
                ahead(q, inner).start()

    def ahead(q, to):
        at = pl.ds((q % 2) * half, half)
        return pltpu.make_async_remote_copy(
            src_ref=piece2.at[at],
            dst_ref=extra.at[at],
            send_sem=e_send.at[q % 2],
            recv_sem=e_recv.at[q % 2],
            device_id={"tensor": to},
            device_id_type=MESH,
        )

    put = []
    tile = 256
    deep = 2 * rows
    tiles = tok.shape[0] // tile

    def product(w, part, mode):
        base = pl.multiple_of(part * deep, deep)
        outs = (out0, out1)
        copy = pltpu.make_async_copy(
            wfull.at[w, pl.ds(base, deep)], outs[w].at[pl.ds(base, deep)], put_sem.at[len(put)]
        )
        copy.start()
        put.append(copy)
        dst = (acc, pre_out)[w]

        def step(i, c):
            at = pl.ds(pl.multiple_of(i * tile, tile), tile)
            value = jnp.dot(
                tok[at, pl.ds(base, deep)],
                wfull[w, pl.ds(base, deep), :],
                preferred_element_type=jnp.float32,
            )
            if mode != "first":
                value = value + dst[at, :]
            if w == 0 and mode == "last":
                x_out[at, :] = value.astype(jnp.bfloat16)
            else:
                dst[at, :] = value
            return c

        lax.fori_loop(0, tiles, step, 0)

    chip, chip_x, chip_y, chip_d = f // 2, xp // 2, yp // 2, diag // 2

    first(0)
    first(1)
    relay(0)
    first(2)
    arrive(6)
    for h in range(2):
        for g in range(gfull.shape[0]):
            for b in range(per):
                at = pl.ds(pl.multiple_of((f * 2 + h) * ghalf, ghalf), ghalf)
                gfull[g, b, at, :] = jnp.concatenate(
                    [gheld[s, g, b, h * ghalf : (h + 1) * ghalf, :] for s in range(zs)], axis=1
                )
    first(4)
    first(5)
    relay(1)
    first(3)
    tok_copy.wait()
    have(0, 2)
    have(1, 2)
    product(0, chip, "first")
    across(0)
    relay(2)
    have(0, 4)
    have(1, 4)
    product(0, chip_x, "more")
    relay(4)
    relay(5)
    first_out(4)
    across(1)
    have(0, 5)
    have(1, 5)
    product(0, chip_y, "more")
    relay(3)
    have(0, 6)
    have(1, 6)
    product(0, chip_d, "last")
    first_out(5)
    for q in (4, 5, 2):
        across(q)
    have(2, 2)
    have(3, 2)
    product(1, chip, "first")
    have(2, 4)
    have(3, 4)
    product(1, chip_x, "more")
    across(3)
    have(2, 5)
    have(3, 5)
    product(1, chip_y, "more")
    for q in (4, 5):
        have(q, 2, 4, 5, 6)
    for g in range(gfull.shape[0]):
        for b in range(per):
            gates_out[g, b] = gfull[g, b].T
    have(2, 6)
    have(3, 6)
    product(1, chip_d, "last")
    for end, inner in ((0, 1), (zs - 1, zs - 2)):
        @pl.when(z == end)
        def _():
            for q in (4, 5):
                ahead(q, inner).wait_send()

        @pl.when(z == inner)
        def _():
            for q in (4, 5):
                ahead(q, end).wait_recv()

    for copy in put:
        copy.wait()
    drain(range(6))
    for q in range(7):
        for k in range(1, zs):
            a2a[q, k].wait_send()


def spread(order, sources, gates, tokens, zs, fs):
    chan, blocks, rows = sources[0].shape
    kinds, _, gin, gout = gates.shape
    per = blocks // zs
    width = per * chan * zs
    toks = tokens.shape[0]
    full = jax.ShapeDtypeStruct((rows * fs, width), jnp.bfloat16)
    vmem = pl.BlockSpec(memory_space=pltpu.VMEM)
    hbm = pl.BlockSpec(memory_space=pl.ANY)
    dma = pltpu.SemaphoreType.DMA
    return pl.pallas_call(
        spread_body,
        in_specs=[pl.BlockSpec(memory_space=pltpu.SMEM)] + [vmem] * 4 + [hbm],
        out_specs=[hbm, hbm, vmem, vmem, vmem, vmem, vmem],
        out_shape=[
            full,
            full,
            jax.ShapeDtypeStruct((rows, width), jnp.bfloat16),
            jax.ShapeDtypeStruct((rows, width), jnp.bfloat16),
            jax.ShapeDtypeStruct((kinds, per, gout * zs, gin * fs), jnp.bfloat16),
            jax.ShapeDtypeStruct((toks, width), jnp.bfloat16),
            jax.ShapeDtypeStruct((toks, width), jnp.float32),
        ],
        scratch_shapes=[
            pltpu.VMEM((chan * blocks, chan * blocks), jnp.bfloat16),
            pltpu.VMEM((chan * blocks, rows), jnp.bfloat16),
            pltpu.VMEM((3, blocks, chan, rows), jnp.bfloat16),
            pltpu.VMEM((kinds, blocks, gin, gout), jnp.bfloat16),
            pltpu.VMEM((3, zs, per, chan, rows), jnp.bfloat16),
            pltpu.VMEM((zs, kinds, per, gin, gout), jnp.bfloat16),
            pltpu.VMEM((kinds, per, gin * fs, gout * zs), jnp.bfloat16),
            pltpu.VMEM((2, rows * fs, width), jnp.bfloat16),
            pltpu.VMEM(tokens.shape, jnp.bfloat16),
            pltpu.VMEM((toks, width), jnp.float32),
            dma,
            dma((7,)),
            dma((7, zs)),
            dma((7, zs)),
            dma((2,)),
            dma((2,)),
            dma((8,)),
            dma((6, 7)),
            dma((6, 7)),
        ],
        compiler_params=pltpu.CompilerParams(
            collective_id=0, has_side_effects=True, vmem_limit_bytes=VMEM_LIMIT
        ),
        name="spread",
    )(order, *sources, gates, tokens)


def chain_body(
    gated, piece, extra, out, mixed,
    wfull, wend, rows_in, early_out, early_right, early_left, late_out, late_right, late_left,
    put_sem, r_send, r_recv, l_send, l_recv, f_send, f_recv,
):
    z = lax.axis_index("tensor")
    zs = lax.axis_size("tensor")
    f, sib, xp, yp, diag = places()
    rows = piece.shape[0]
    parts = 4
    part = rows // parts
    cut, rt = early_out.shape[2], early_out.shape[1]
    wide, lt = late_out.shape[3], late_out.shape[2]
    cuts = wfull.shape[0] // cut
    quarter = cuts // zs
    halves = rows // cut
    late = (gated.shape[0] - rt) // lt
    inner = (z > 0) & (z < zs - 1)
    mine = pl.ds(pl.multiple_of(f * rows, rows), rows)
    wfull[mine, :] = piece[...]
    wend[mine, :] = extra[...]
    greet(zs, z, (sib, xp, yp))

    def view(q, owner):
        to = wfull if q < parts else wend
        return to.at[pl.ds(owner * rows + (q % parts) * part, part)]

    first, relay, across, have, drain = gatherer(view, f_send, f_recv)

    def dot(x, w, at):
        return lax.dot_general(x, w[at, :], NT, preferred_element_type=jnp.float32)

    def early_term(d):
        return dot(gated[:rt, :], wfull, pl.ds(d * cut, cut))

    def late_rows(t):
        return slice(rt + t * lt, rt + (t + 1) * lt)

    def late_term(t, q):
        return dot(gated[late_rows(t), :], wfull, pl.ds(q * wide, wide))

    def end_term(t, q):
        return dot(rows_in[t * lt : (t + 1) * lt, :], wend, pl.ds(q * wide, wide))

    def move(src, dst, s, forward):
        return pltpu.make_async_remote_copy(
            src_ref=src,
            dst_ref=dst,
            send_sem=(r_send if forward else l_send).at[s],
            recv_sem=(r_recv if forward else l_recv).at[s],
            device_id={"tensor": (z + (1 if forward else zs - 1)) % zs},
            device_id_type=MESH,
        )

    def early_move(d, forward):
        ins = early_right if forward else early_left
        return move(early_out.at[d], ins.at[d], d, forward)

    def late_move(t, q, forward):
        ins = late_right if forward else late_left
        return move(late_out.at[q, t], ins.at[q, t], cuts + q * late + t, forward)

    def row_move(t, forward):
        return move(
            gated.at[pl.ds(rt + t * lt, lt)], rows_in.at[pl.ds(t * lt, lt)],
            cuts + zs * late + t, forward,
        )

    def ordered(q):
        return sorted(range(q * quarter, (q + 1) * quarter), key=lambda d: (d % halves, d))

    lists = {}
    for forward in (True, False):
        far = range(zs - 1, 0, -1) if forward else range(zs - 1)
        groups = [[("early", d) for d in ordered(q)] for q in far]
        groups.insert(zs - 2, [("rows", t) for t in range(late)])
        lists[forward] = [item for group in groups for item in group]

    def one(forward, k):
        kind, n = lists[forward][k]
        return early_move(n, forward) if kind == "early" else row_move(n, forward)

    def early_pass(d, forward):
        value = early_term(d)
        early_move(d, forward).wait_recv()
        ins = early_right if forward else early_left
        early_out[d] = (value + ins[d].astype(jnp.float32)).astype(jnp.bfloat16)
        early_move(d, forward).start()

    def late_pass(t, q, forward):
        value = late_term(t, q)
        late_move(t, q, forward).wait_recv()
        ins = late_right if forward else late_left
        late_out[q, t] = (value + ins[q, t].astype(jnp.float32)).astype(jnp.bfloat16)
        late_move(t, q, forward).start()

    def end(forward, away):
        return z == (away if forward else zs - 1 - away)

    def beyond(forward, away):
        return range(zs - 1, away, -1) if forward else range(zs - 1 - away)

    def step(k):
        for forward in (True, False):
            kind, n = lists[forward][k]

            @pl.when(end(forward, 0))
            def _():
                if kind == "early":
                    early_out[n] = early_term(n).astype(jnp.bfloat16)
                if k >= 2:
                    one(forward, k - 2).wait_send()
                one(forward, k).start()

            if kind == "rows":
                @pl.when(end(forward, 1))
                def _():
                    row_move(n, forward).wait_recv()
                    for q in beyond(forward, 1):
                        late_out[q, n] = (late_term(n, q) + end_term(n, q)).astype(jnp.bfloat16)
                        late_move(n, q, forward).start()

        for forward in (True, False):
            kind, n = lists[forward][k]
            for away in range(1, zs - 1):
                if kind == "early":
                    if n // quarter in beyond(forward, away):
                        @pl.when(end(forward, away))
                        def _():
                            early_pass(n, forward)
                elif away > 1:
                    @pl.when(end(forward, away))
                    def _():
                        for q in beyond(forward, away):
                            late_pass(n, q, forward)

    def all_of(q):
        have(q, 2, 4, 5, 6)

    def when_inner(*acts):
        @pl.when(inner)
        def _():
            for act, q in acts:
                act(q)

    for q in range(parts):
        first(q)
    relay(0)
    relay(1)
    across(0)
    across(1)
    all_of(0)
    all_of(1)
    step(0)
    relay(2)
    relay(3)
    step(1)
    across(2)
    across(3)
    when_inner(*((first, parts + q) for q in range(parts)))
    all_of(2)
    all_of(3)
    put = pltpu.make_async_copy(wfull, out, put_sem)
    put.start()
    step(2)
    step(3)
    when_inner((relay, parts), (relay, parts + 1))
    step(4)
    when_inner((relay, parts + 2), (across, parts), (across, parts + 1))
    step(5)
    when_inner((relay, parts + 3), (across, parts + 2))
    step(6)
    when_inner((across, parts + 3))
    step(7)
    when_inner(*((all_of, parts + q) for q in range(parts)))
    for k in range(8, len(lists[True])):
        step(k)

    for c in range(zs):
        @pl.when(z == c)
        def _():
            for t in range(late):
                value = late_term(t, c)
                if c in (1, zs - 2):
                    value = value + end_term(t, c)
                if c > 1:
                    late_move(t, c, True).wait_recv()
                    value = value + late_right[c, t].astype(jnp.float32)
                if c < zs - 2:
                    late_move(t, c, False).wait_recv()
                    value = value + late_left[c, t].astype(jnp.float32)
                mixed[late_rows(t), :] = value.astype(mixed.dtype)
            for d in ordered(c):
                value = early_term(d)
                if c > 0:
                    early_move(d, True).wait_recv()
                    value = value + early_right[d].astype(jnp.float32)
                if c < zs - 1:
                    early_move(d, False).wait_recv()
                    value = value + early_left[d].astype(jnp.float32)
                e = d - c * quarter
                mixed[:rt, e * cut : (e + 1) * cut] = value.astype(mixed.dtype)
            for forward in (True, False):
                away = c if forward else zs - 1 - c
                if away == 0:
                    for k in range(len(lists[forward]) - 2, len(lists[forward])):
                        one(forward, k).wait_send()
                else:
                    for q in beyond(forward, away):
                        for d in ordered(q):
                            early_move(d, forward).wait_send()
                        for t in range(late):
                            late_move(t, q, forward).wait_send()

    drain(range(parts))
    when_inner((drain, range(parts, 2 * parts)))
    put.wait()


def chain(gated, piece, extra, zs, fs):
    rows, width = piece.shape
    toks = gated.shape[0]
    depth = rows * fs
    cut, rt = rows // 2, toks // 2
    wide, lt = depth // zs, toks // 8
    late = (toks - rt) // lt
    vmem = pl.BlockSpec(memory_space=pltpu.VMEM)
    dma = pltpu.SemaphoreType.DMA
    early_buf = pltpu.VMEM((depth // cut, rt, cut), jnp.bfloat16)
    late_buf = pltpu.VMEM((zs, late, lt, wide), jnp.bfloat16)
    sems = dma((depth // cut + (zs + 1) * late,))
    return pl.pallas_call(
        chain_body,
        in_specs=[vmem, vmem, vmem],
        out_specs=[pl.BlockSpec(memory_space=pl.ANY), vmem],
        out_shape=[
            jax.ShapeDtypeStruct((depth, width), jnp.bfloat16),
            jax.ShapeDtypeStruct((toks, depth // zs), jnp.bfloat16),
        ],
        scratch_shapes=[
            pltpu.VMEM((depth, width), jnp.bfloat16),
            pltpu.VMEM((depth, width), jnp.bfloat16),
            pltpu.VMEM((toks - rt, width), jnp.bfloat16),
            early_buf,
            early_buf,
            early_buf,
            late_buf,
            late_buf,
            late_buf,
            dma,
            sems,
            sems,
            sems,
            sems,
            dma((8, 7)),
            dma((8, 7)),
        ],
        compiler_params=pltpu.CompilerParams(
            collective_id=1, has_side_effects=True, vmem_limit_bytes=VMEM_LIMIT
        ),
        name="chain",
    )(gated, piece, extra)


def dup_body(x_ref, y_ref, x_out, y_out):
    x_out[...] = x_ref[...]
    y_out[...] = y_ref[...]


def dup(x, y):
    steps = 8
    specs = [pl.BlockSpec((a.shape[0] // steps, a.shape[1]), lambda i: (i, 0)) for a in (x, y)]
    return pl.pallas_call(
        dup_body,
        grid=(steps,),
        in_specs=specs,
        out_specs=specs,
        out_shape=[jax.ShapeDtypeStruct(a.shape, a.dtype) for a in (x, y)],
        cost_estimate=pl.CostEstimate(flops=0, bytes_accessed=4 * (x.size + y.size), transcendentals=0),
        name="dup",
    )(x, y)


def on_device(
    tokens, input_source, branch_source, output_source, gates_source, decay_param, block_order
):
    zs, fs = lax.axis_size("tensor"), lax.axis_size("fsdp")
    blocks = block_order.shape[0]
    per_dev = blocks // zs
    prompts = tokens.shape[0] // LEN
    picked = (block_order[:, None] == jnp.arange(blocks)[None, :]).astype(jnp.float32)
    soft = -8.0 * jax.nn.softplus(decay_param)
    own = lax.dynamic_slice_in_dim(picked, lax.axis_index("tensor") * per_dev, per_dev)
    rate = jnp.sum(own[:, :, None] * soft[None, :, :], axis=1)[:, None, :]
    sources = (input_source, branch_source, output_source)
    if fs == 8 and zs == 4:
        wi, wb, piece, extra, gates, branch_in, gate_pre = spread(
            block_order, sources, gates_source, tokens, zs, fs
        )
        gated, wi, wb, gates = recur(branch_in, gate_pre, gates, rate, wi, wb, prompts)
        wo, mixed = chain(gated, piece, extra, zs, fs)
        wo, mixed = dup(wo, mixed)
        return mixed, wi, wb, wo, gates
    hot = picked.astype(jnp.bfloat16)
    sectioned = tuple(
        jnp.einsum(
            "jb,cbr->cjr", hot, s.astype(jnp.bfloat16), preferred_element_type=jnp.float32
        ).astype(jnp.bfloat16)
        for s in sources
    )
    gate_sectioned = jnp.einsum(
        "jb,gbio->gjio", hot, gates_source.astype(jnp.bfloat16), preferred_element_type=jnp.float32
    ).astype(jnp.bfloat16)
    gate_group = lax.all_to_all(gate_sectioned, "tensor", split_axis=1, concat_axis=3, tiled=True)
    gates = lax.all_gather(jnp.transpose(gate_group, (0, 1, 3, 2)), "fsdp", axis=3, tiled=True)
    regrouped = lax.all_to_all(sectioned, "tensor", split_axis=1, concat_axis=0, tiled=True)
    wi, wb, wo = (
        lax.all_gather(
            jnp.transpose(w, (2, 1, 0)).reshape(w.shape[2], -1), "fsdp", axis=0, tiled=True
        )
        for w in regrouped
    )
    branch_in = jnp.dot(tokens, wi, preferred_element_type=jnp.float32).astype(jnp.bfloat16)
    gate_pre = jnp.dot(tokens, wb, preferred_element_type=jnp.float32)
    gated, wi, wb, gates = recur(branch_in, gate_pre, gates, rate, wi, wb, prompts)
    partial_value = lax.dot_general(gated, wo, NT, preferred_element_type=jnp.float32)
    mixed = lax.psum_scatter(
        partial_value.astype(jnp.bfloat16), "tensor", scatter_dimension=1, tiled=True
    )
    return mixed, wi, wb, wo, gates


def solution(mesh):
    return jax.shard_map(
        on_device,
        mesh=mesh,
        in_specs=(
            P("fsdp", None),
            P("tensor", None, "fsdp"),
            P("tensor", None, "fsdp"),
            P("tensor", None, "fsdp"),
            P(None, None, "fsdp", "tensor"),
            P(),
            P(),
        ),
        out_specs=(
            P("fsdp", "tensor"),
            P(None, "tensor"),
            P(None, "tensor"),
            P(None, "tensor"),
            P(None, "tensor", None, None),
        ),
        check_vma=False,
    )
```

```python
import functools
import jax
import jax.numpy as jnp
from jax import lax
from jax.experimental import pallas as pl
from jax.experimental.pallas import tpu as pltpu
from jax.sharding import PartitionSpec as P

LEN = 256
SUB = 8
VMEM_LIMIT = 60 * 2**20
MESH = pl.DeviceIdType.MESH
NT = (((1,), (1,)), ((), ()))


def recur_body(
    prompts, x_ref, pre_ref, g_ref, r_ref, wi_ref, wb_ref,
    o_ref, wi_out, wb_out, g_out, a_s, d_s, carry,
):
    @pl.when(pl.program_id(1) == 0)
    def _():
        carry[...] = jnp.zeros_like(carry)
        g_out[...] = g_ref[...]

    wi_out[...] = wi_ref[...]
    wb_out[...] = wb_ref[...]
    x = x_ref[...]
    pre_r = lax.dot_general(x, g_ref[0, 0], NT, preferred_element_type=jnp.float32)
    pre_i = lax.dot_general(x, g_ref[1, 0], NT, preferred_element_type=jnp.float32)
    a = jnp.exp(r_ref[0] * jax.nn.sigmoid(pre_r))
    a_s[...] = a
    d_s[...] = jnp.sqrt(jnp.maximum(1.0 - a * a, 0.0)) * (
        jax.nn.sigmoid(pre_i) * x.astype(jnp.float32)
    )
    rows, chan = a_s.shape
    group = lax.broadcasted_iota(jnp.int32, (SUB, chan), 0) // prompts

    def last(v):
        res = v
        for g in range(SUB // prompts - 1):
            res = jnp.where(group == g, pltpu.roll(v, (g + 1) * prompts, 0), res)
        return res

    def step(i, c):
        at = pl.ds(pl.multiple_of(i * SUB, SUB), SUB)
        a = a_s[at, :]
        d = d_s[at, :]
        shift = 1
        while shift < SUB // prompts:
            a_sh = pltpu.roll(a, shift * prompts, 0)
            d_sh = pltpu.roll(d, shift * prompts, 0)
            d = jnp.where(group >= shift, a * d_sh + d, d)
            a = jnp.where(group >= shift, a * a_sh, a)
            shift *= 2
        d_s[at, :] = a * c + d
        return last(a) * c + last(d)

    carry[...] = lax.fori_loop(0, rows // SUB, step, carry[...], unroll=8)
    o_ref[...] = (d_s[...] * jax.nn.gelu(pre_ref[...], approximate=True)).astype(o_ref.dtype)


def recur(branch_in, gate_pre, gates, rate, wi, wb, prompts):
    rows, width = branch_in.shape
    blocks, chan = gates.shape[1], gates.shape[2]
    tile = min(rows, 256)
    tiles = rows // tile
    part = wi.shape[0] // (blocks * tiles)
    cell = pl.BlockSpec((tile, chan), lambda b, t: (t, b))
    gate = pl.BlockSpec((2, 1, chan, chan), lambda b, t: (0, b, 0, 0))
    slab = pl.BlockSpec((part, width), lambda b, t: (b * tiles + t, 0))
    return pl.pallas_call(
        functools.partial(recur_body, prompts),
        grid=(blocks, tiles),
        in_specs=[cell, cell, gate, pl.BlockSpec((1, 1, chan), lambda b, t: (b, 0, 0)), slab, slab],
        out_specs=[cell, slab, slab, gate],
        out_shape=[
            jax.ShapeDtypeStruct((rows, width), jnp.bfloat16),
            jax.ShapeDtypeStruct(wi.shape, wi.dtype),
            jax.ShapeDtypeStruct(wb.shape, wb.dtype),
            jax.ShapeDtypeStruct(gates.shape, gates.dtype),
        ],
        scratch_shapes=[
            pltpu.VMEM((tile, chan), jnp.float32),
            pltpu.VMEM((tile, chan), jnp.float32),
            pltpu.VMEM((SUB, chan), jnp.float32),
        ],
        compiler_params=pltpu.CompilerParams(
            dimension_semantics=("arbitrary", "arbitrary"), vmem_limit_bytes=VMEM_LIMIT
        ),
        cost_estimate=pl.CostEstimate(
            flops=4 * rows * width * chan, bytes_accessed=8 * rows * width, transcendentals=6 * rows * width
        ),
        name="recur",
    )(branch_in, gate_pre, gates, rate, wi, wb)


def places():
    f = lax.axis_index("fsdp")
    sib = f + 1 - 2 * (f % 2)
    xp = f + 2 - 4 * ((f // 2) % 2)
    yp = f + 4 - 8 * (f // 4)
    diag = xp + 4 - 8 * (xp // 4)
    return f, sib, xp, yp, diag


def greet(zs, z, peers):
    barrier = pltpu.get_barrier_semaphore()
    for peer in peers:
        pl.semaphore_signal(barrier, inc=1, device_id={"fsdp": peer}, device_id_type=MESH)
    for k in range(1, zs):
        pl.semaphore_signal(
            barrier, inc=1, device_id={"tensor": (z + k) % zs}, device_id_type=MESH
        )
    pl.semaphore_wait(barrier, len(peers) + zs - 1)


def gatherer(view, f_send, f_recv):
    f, sib, xp, yp, diag = places()

    def make(q, i):
        near, far = ((xp, yp), (yp, xp))[q % 2]
        owner, peer = (
            (f, xp), (f, yp), (f, sib), (near, far), (xp, sib), (yp, sib), (diag, sib),
        )[i]
        at = view(q, owner)
        return pltpu.make_async_remote_copy(
            src_ref=at,
            dst_ref=at,
            send_sem=f_send.at[q, i],
            recv_sem=f_recv.at[q, i],
            device_id={"fsdp": peer},
            device_id_type=MESH,
        )

    def first(q):
        for i in range(3):
            make(q, i).start()

    def relay(q):
        make(q, 0).wait_recv()
        if q % 2 == 0:
            make(q, 3).start()
        make(q, 4).start()
        make(q, 1).wait_recv()
        if q % 2 == 1:
            make(q, 3).start()
        make(q, 5).start()

    def across(q):
        make(q, 3).wait_recv()
        make(q, 6).start()

    def have(q, *ways):
        for i in ways:
            make(q, i).wait_recv()

    def hand(q):
        for i in (3, 4, 5):
            make(q, i).start()

    def drain(qs, ways=range(7)):
        for q in qs:
            for i in ways:
                make(q, i).wait_send()

    return first, relay, across, have, drain, hand


def spread_body(
    order, src0, src1, src2, gsrc, tokens,
    out0, out1, piece2, extra, gates_out, x_out, pre_out,
    perm, xb, sbuf, gsend, held, gheld, gfull, wfull, tok, acc,
    tok_sem, own_sem, z_send, z_recv, e_send, e_recv, put_sem, f_send, f_recv,
):
    srcs = (src0, src1, src2)
    z = lax.axis_index("tensor")
    f, sib, xp, yp, diag = places()
    zs, per, chan = held.shape[1], held.shape[2], held.shape[3]
    rows = held.shape[4]
    half = rows // 2
    ghalf = gheld.shape[3] // 2
    group = per * chan
    tok_copy = pltpu.make_async_copy(tokens, tok, tok_sem)
    tok_copy.start()

    def cast(w):
        xb[...] = srcs[w][...].reshape(xb.shape).astype(jnp.bfloat16)
        for k in range(zs):
            part = jnp.dot(
                perm[k * group : (k + 1) * group, :], xb[...], preferred_element_type=jnp.float32
            )
            sbuf[w, k * per : (k + 1) * per] = part.astype(jnp.bfloat16).reshape(per, chan, rows)

    blocks = sbuf.shape[1]
    column = lax.broadcasted_iota(jnp.int32, (chan, perm.shape[1]), 1)
    channel = lax.broadcasted_iota(jnp.int32, (chan, perm.shape[1]), 0) * blocks
    for j in range(blocks):
        perm[j * chan : (j + 1) * chan, :] = jnp.where(
            column == channel + order[j], 1.0, 0.0
        ).astype(jnp.bfloat16)
    cast(0)
    greet(zs, z, (sib, xp, yp))

    def z_source(q, to):
        if q == 6:
            return gsend.at[:, pl.ds(to * per, per)]
        return sbuf.at[q // 2, pl.ds(to * per, per), :, pl.ds((q % 2) * half, half)]

    def z_target(q):
        if q == 6:
            return gheld.at[z]
        return held.at[q // 2, z, :, :, pl.ds((q % 2) * half, half)]

    a2a, own = {}, {}
    queue = [0, 1, 2, 6, 3, 4, 5]

    def depart():
        q = queue.pop(0)
        for k in range(1, zs):
            to = (z + k) % zs
            a2a[q, k] = pltpu.make_async_remote_copy(
                src_ref=z_source(q, to),
                dst_ref=z_target(q),
                send_sem=z_send.at[q, k],
                recv_sem=z_recv.at[q, k],
                device_id={"tensor": to},
                device_id_type=MESH,
            )
            a2a[q, k].start()
        own[q] = pltpu.make_async_copy(z_source(q, z), z_target(q), own_sem.at[q])
        own[q].start()

    depart()
    cast(1)
    cast(2)
    for g in range(gsend.shape[0]):
        for j in range(gsend.shape[1]):
            gsend[g, j] = gsrc[g, order[j]].astype(jnp.bfloat16)

    def arrive(q):
        own[q].wait()
        for k in range(1, zs):
            a2a[q, k].wait_recv()
        for _ in range(2 if q == 0 else 1):
            if queue:
                depart()

    def slab(q, b):
        at = slice((q % 2) * half, (q % 2) * half + half)
        return jnp.concatenate([held[q // 2, s, b, :, at] for s in range(zs)], axis=0).T

    def view(q, owner):
        if q >= 4:
            return gfull.at[:, :, pl.ds(owner * 2 * ghalf + (q - 4) * ghalf, ghalf)]
        return wfull.at[q // 2, pl.ds(owner * rows + (q % 2) * half, half)]

    send_first, relay, across, have, drain, _ = gatherer(view, f_send, f_recv)

    def first(q):
        if q < 4:
            arrive(q)
            at = pl.ds(pl.multiple_of(f * rows + (q % 2) * half, half), half)
            for b in range(per):
                width = chan * zs
                wfull[q // 2, at, b * width : (b + 1) * width] = slab(q, b)
        send_first(q)

    def first_out(q):
        arrive(q)
        at = slice((q % 2) * half, (q % 2) * half + half)
        for b in range(per):
            width = chan * zs
            piece2[at, b * width : (b + 1) * width] = slab(q, b)
        for end, inner in ((0, 1), (zs - 1, zs - 2)):
            @pl.when(z == end)
            def _():
                ahead(q, inner).start()

    def ahead(q, to):
        at = pl.ds((q % 2) * half, half)
        return pltpu.make_async_remote_copy(
            src_ref=piece2.at[at],
            dst_ref=extra.at[at],
            send_sem=e_send.at[q % 2],
            recv_sem=e_recv.at[q % 2],
            device_id={"tensor": to},
            device_id_type=MESH,
        )

    put = []
    tile = 256
    deep = 2 * rows
    tiles = tok.shape[0] // tile

    def product(w, part, mode):
        base = pl.multiple_of(part * deep, deep)
        outs = (out0, out1)
        copy = pltpu.make_async_copy(
            wfull.at[w, pl.ds(base, deep)], outs[w].at[pl.ds(base, deep)], put_sem.at[len(put)]
        )
        copy.start()
        put.append(copy)
        dst = (acc, pre_out)[w]

        def step(i, c):
            at = pl.ds(pl.multiple_of(i * tile, tile), tile)
            value = jnp.dot(
                tok[at, pl.ds(base, deep)],
                wfull[w, pl.ds(base, deep), :],
                preferred_element_type=jnp.float32,
            )
            if mode != "first":
                value = value + dst[at, :]
            if w == 0 and mode == "last":
                x_out[at, :] = value.astype(jnp.bfloat16)
            else:
                dst[at, :] = value
            return c

        lax.fori_loop(0, tiles, step, 0)

    chip, chip_x, chip_y, chip_d = f // 2, xp // 2, yp // 2, diag // 2

    first(0)
    first(1)
    relay(0)
    first(2)
    arrive(6)
    for h in range(2):
        for g in range(gfull.shape[0]):
            for b in range(per):
                at = pl.ds(pl.multiple_of((f * 2 + h) * ghalf, ghalf), ghalf)
                gfull[g, b, at, :] = jnp.concatenate(
                    [gheld[s, g, b, h * ghalf : (h + 1) * ghalf, :] for s in range(zs)], axis=1
                )
    first(4)
    first(5)
    relay(1)
    first(3)
    tok_copy.wait()
    have(0, 2)
    have(1, 2)
    product(0, chip, "first")
    across(0)
    relay(2)
    have(0, 4)
    have(1, 4)
    product(0, chip_x, "more")
    relay(4)
    relay(5)
    first_out(4)
    across(1)
    have(0, 5)
    have(1, 5)
    product(0, chip_y, "more")
    relay(3)
    have(0, 6)
    have(1, 6)
    product(0, chip_d, "last")
    first_out(5)
    for q in (4, 5, 2):
        across(q)
    have(2, 2)
    have(3, 2)
    product(1, chip, "first")
    have(2, 4)
    have(3, 4)
    product(1, chip_x, "more")
    across(3)
    have(2, 5)
    have(3, 5)
    product(1, chip_y, "more")
    for q in (4, 5):
        have(q, 2, 4, 5, 6)
    for g in range(gfull.shape[0]):
        for b in range(per):
            gates_out[g, b] = gfull[g, b].T
    have(2, 6)
    have(3, 6)
    product(1, chip_d, "last")
    for end, inner in ((0, 1), (zs - 1, zs - 2)):
        @pl.when(z == end)
        def _():
            for q in (4, 5):
                ahead(q, inner).wait_send()

        @pl.when(z == inner)
        def _():
            for q in (4, 5):
                ahead(q, end).wait_recv()

    for copy in put:
        copy.wait()
    drain(range(6))
    for q in range(7):
        for k in range(1, zs):
            a2a[q, k].wait_send()


def spread(order, sources, gates, tokens, zs, fs):
    chan, blocks, rows = sources[0].shape
    kinds, _, gin, gout = gates.shape
    per = blocks // zs
    width = per * chan * zs
    toks = tokens.shape[0]
    full = jax.ShapeDtypeStruct((rows * fs, width), jnp.bfloat16)
    vmem = pl.BlockSpec(memory_space=pltpu.VMEM)
    hbm = pl.BlockSpec(memory_space=pl.ANY)
    dma = pltpu.SemaphoreType.DMA
    return pl.pallas_call(
        spread_body,
        in_specs=[pl.BlockSpec(memory_space=pltpu.SMEM)] + [vmem] * 4 + [hbm],
        out_specs=[hbm, hbm, vmem, vmem, vmem, vmem, vmem],
        out_shape=[
            full,
            full,
            jax.ShapeDtypeStruct((rows, width), jnp.bfloat16),
            jax.ShapeDtypeStruct((rows, width), jnp.bfloat16),
            jax.ShapeDtypeStruct((kinds, per, gout * zs, gin * fs), jnp.bfloat16),
            jax.ShapeDtypeStruct((toks, width), jnp.bfloat16),
            jax.ShapeDtypeStruct((toks, width), jnp.float32),
        ],
        scratch_shapes=[
            pltpu.VMEM((chan * blocks, chan * blocks), jnp.bfloat16),
            pltpu.VMEM((chan * blocks, rows), jnp.bfloat16),
            pltpu.VMEM((3, blocks, chan, rows), jnp.bfloat16),
            pltpu.VMEM((kinds, blocks, gin, gout), jnp.bfloat16),
            pltpu.VMEM((3, zs, per, chan, rows), jnp.bfloat16),
            pltpu.VMEM((zs, kinds, per, gin, gout), jnp.bfloat16),
            pltpu.VMEM((kinds, per, gin * fs, gout * zs), jnp.bfloat16),
            pltpu.VMEM((2, rows * fs, width), jnp.bfloat16),
            pltpu.VMEM(tokens.shape, jnp.bfloat16),
            pltpu.VMEM((toks, width), jnp.float32),
            dma,
            dma((7,)),
            dma((7, zs)),
            dma((7, zs)),
            dma((2,)),
            dma((2,)),
            dma((8,)),
            dma((6, 7)),
            dma((6, 7)),
        ],
        compiler_params=pltpu.CompilerParams(
            collective_id=0, has_side_effects=True, vmem_limit_bytes=VMEM_LIMIT
        ),
        name="spread",
    )(order, *sources, gates, tokens)


def chain_body(
    gated, piece, piece_x, piece_y, piece_s, extra, out, mixed,
    wfull, wend, rows_in, early_out, early_right, early_left, late_out, late_right, late_left,
    put_sem, get_sem, r_send, r_recv, l_send, l_recv, f_send, f_recv,
):
    z = lax.axis_index("tensor")
    zs = lax.axis_size("tensor")
    f, sib, xp, yp, diag = places()
    rows = piece.shape[0]
    parts = 4
    part = rows // parts
    cut, rt = early_out.shape[2], early_out.shape[1]
    wide, lt = late_out.shape[3], late_out.shape[2]
    cuts = wfull.shape[0] // cut
    quarter = cuts // zs
    halves = rows // cut
    late = (gated.shape[0] - rt) // lt
    inner = (z > 0) & (z < zs - 1)
    gets = []
    for ref, to, owner in (
        (piece_x, wfull, xp), (piece_y, wfull, yp), (piece, wfull, f), (piece_s, wfull, sib), (extra, wend, f),
    ):
        at = pl.ds(pl.multiple_of(owner * rows, rows), rows)
        gets.append(pltpu.make_async_copy(ref, to.at[at], get_sem.at[len(gets)]))
        gets[-1].start()
    greet(zs, z, (sib, xp, yp))

    def view(q, owner):
        to = wfull if q < parts else wend
        return to.at[pl.ds(owner * rows + (q % parts) * part, part)]

    first, relay, across, have, drain, hand = gatherer(view, f_send, f_recv)

    def dot(x, w, at):
        return lax.dot_general(x, w[at, :], NT, preferred_element_type=jnp.float32)

    def early_term(d):
        return dot(gated[:rt, :], wfull, pl.ds(d * cut, cut))

    def late_rows(t):
        return slice(rt + t * lt, rt + (t + 1) * lt)

    def late_term(t, q):
        return dot(gated[late_rows(t), :], wfull, pl.ds(q * wide, wide))

    def end_term(t, q):
        return dot(rows_in[t * lt : (t + 1) * lt, :], wend, pl.ds(q * wide, wide))

    def move(src, dst, s, forward):
        return pltpu.make_async_remote_copy(
            src_ref=src,
            dst_ref=dst,
            send_sem=(r_send if forward else l_send).at[s],
            recv_sem=(r_recv if forward else l_recv).at[s],
            device_id={"tensor": (z + (1 if forward else zs - 1)) % zs},
            device_id_type=MESH,
        )

    def early_move(d, forward):
        ins = early_right if forward else early_left
        return move(early_out.at[d], ins.at[d], d, forward)

    def late_move(t, q, forward):
        ins = late_right if forward else late_left
        return move(late_out.at[q, t], ins.at[q, t], cuts + q * late + t, forward)

    def row_move(t, forward):
        return move(
            gated.at[pl.ds(rt + t * lt, lt)], rows_in.at[pl.ds(t * lt, lt)],
            cuts + zs * late + t, forward,
        )

    def ordered(q):
        return sorted(range(q * quarter, (q + 1) * quarter), key=lambda d: (d % halves, d))

    lists, sends = {}, {}
    for forward in (True, False):
        far = range(zs - 1, 0, -1) if forward else range(zs - 1)
        groups = [[("early", d) for d in ordered(q)] for q in far]
        groups.insert(zs - 2, [("rows", t) for t in range(late)])
        lists[forward] = [item for group in groups for item in group]
        start = lists[forward].index(("rows", 0))
        sends[forward] = list(lists[forward])
        sends[forward].insert(0, sends[forward].pop(start))

    def one(forward, k):
        kind, n = sends[forward][k]
        return early_move(n, forward) if kind == "early" else row_move(n, forward)

    def early_pass(d, forward):
        value = early_term(d)
        early_move(d, forward).wait_recv()
        ins = early_right if forward else early_left
        early_out[d] = (value + ins[d].astype(jnp.float32)).astype(jnp.bfloat16)
        early_move(d, forward).start()

    def late_pass(t, q, forward):
        value = late_term(t, q)
        late_move(t, q, forward).wait_recv()
        ins = late_right if forward else late_left
        late_out[q, t] = (value + ins[q, t].astype(jnp.float32)).astype(jnp.bfloat16)
        late_move(t, q, forward).start()

    def end(forward, away):
        return z == (away if forward else zs - 1 - away)

    def beyond(forward, away):
        return range(zs - 1, away, -1) if forward else range(zs - 1 - away)

    def step(k):
        for forward in (True, False):
            given, m = sends[forward][k]

            @pl.when(end(forward, 0))
            def _():
                if given == "early":
                    early_out[m] = early_term(m).astype(jnp.bfloat16)
                if k >= 2:
                    one(forward, k - 2).wait_send()
                one(forward, k).start()

            kind, n = lists[forward][k]
            if kind == "rows":
                @pl.when(end(forward, 1))
                def _():
                    row_move(n, forward).wait_recv()
                    for q in beyond(forward, 1):
                        late_out[q, n] = (late_term(n, q) + end_term(n, q)).astype(jnp.bfloat16)
                        late_move(n, q, forward).start()

        for forward in (True, False):
            kind, n = lists[forward][k]
            for away in range(1, zs - 1):
                if kind == "early":
                    if n // quarter in beyond(forward, away):
                        @pl.when(end(forward, away))
                        def _():
                            early_pass(n, forward)
                elif away > 1:
                    @pl.when(end(forward, away))
                    def _():
                        for q in beyond(forward, away):
                            late_pass(n, q, forward)

    def all_of(q):
        have(q, 2, 4, 5, 6)

    def when_inner(*acts):
        @pl.when(inner)
        def _():
            for act, q in acts:
                act(q)

    def last_late(c, t):
        value = late_term(t, c)
        if c in (1, zs - 2):
            value = value + end_term(t, c)
        if c > 1:
            late_move(t, c, True).wait_recv()
            value = value + late_right[c, t].astype(jnp.float32)
        if c < zs - 2:
            late_move(t, c, False).wait_recv()
            value = value + late_left[c, t].astype(jnp.float32)
        mixed[late_rows(t), :] = value.astype(mixed.dtype)

    def last_early(c, d):
        value = early_term(d)
        if c < zs - 1:
            early_move(d, False).wait_recv()
            value = value + early_left[d].astype(jnp.float32)
        if c > 0:
            early_move(d, True).wait_recv()
            value = value + early_right[d].astype(jnp.float32)
        e = d - c * quarter
        mixed[:rt, e * cut : (e + 1) * cut] = value.astype(mixed.dtype)

    def on_each(cs, act):
        for c in cs:
            @pl.when(z == c)
            def _():
                act(c)

    for get in gets[:2]:
        get.wait()
    hand(0)
    hand(1)
    for get in gets[2:]:
        get.wait()
    across(0)
    across(1)
    hand(2)
    hand(3)
    when_inner((first, parts), (first, parts + 1))
    have(0, 4, 5, 6)
    have(1, 4, 5, 6)
    step(0)
    across(2)
    across(3)
    step(1)
    have(2, 4, 5, 6)
    have(3, 4, 5, 6)
    put = pltpu.make_async_copy(wfull, out, put_sem)
    put.start()
    when_inner((relay, parts), (relay, parts + 1), (first, parts + 2), (first, parts + 3))
    step(2)
    step(3)
    when_inner((across, parts), (across, parts + 1))
    step(4)
    when_inner((relay, parts + 2), (relay, parts + 3))
    step(5)
    step(6)
    when_inner((across, parts + 2), (across, parts + 3))
    step(7)
    when_inner(*((all_of, parts + q) for q in range(parts)))
    count = len(lists[True])
    ends = (0, zs - 1)
    for k in range(8, count):
        step(k)
        if k < 8 + quarter:
            on_each(ends, lambda c: last_early(c, ordered(c)[k - 8]))
        if k >= count - late:
            on_each(range(zs), lambda c: last_late(c, k - count + late))

    for c in range(zs):
        @pl.when(z == c)
        def _():
            if c not in ends:
                for d in ordered(c):
                    last_early(c, d)
            for forward in (True, False):
                away = c if forward else zs - 1 - c
                if away == 0:
                    for k in range(count - 2, count):
                        one(forward, k).wait_send()
                else:
                    for q in beyond(forward, away):
                        for d in ordered(q):
                            early_move(d, forward).wait_send()
                        for t in range(late):
                            late_move(t, q, forward).wait_send()

    drain(range(parts), range(3, 7))
    when_inner((drain, range(parts, 2 * parts)))
    put.wait()


def chain(gated, piece, near, extra, zs, fs):
    rows, width = piece.shape
    toks = gated.shape[0]
    depth = rows * fs
    cut, rt = rows // 2, toks // 2
    wide, lt = depth // zs, toks // 8
    late = (toks - rt) // lt
    vmem = pl.BlockSpec(memory_space=pltpu.VMEM)
    hbm = pl.BlockSpec(memory_space=pl.ANY)
    dma = pltpu.SemaphoreType.DMA
    early_buf = pltpu.VMEM((depth // cut, rt, cut), jnp.bfloat16)
    late_buf = pltpu.VMEM((zs, late, lt, wide), jnp.bfloat16)
    sems = dma((depth // cut + (zs + 1) * late,))
    return pl.pallas_call(
        chain_body,
        in_specs=[vmem] + [hbm] * 5,
        out_specs=[hbm, vmem],
        out_shape=[
            jax.ShapeDtypeStruct((depth, width), jnp.bfloat16),
            jax.ShapeDtypeStruct((toks, depth // zs), jnp.bfloat16),
        ],
        scratch_shapes=[
            pltpu.VMEM((depth, width), jnp.bfloat16),
            pltpu.VMEM((depth, width), jnp.bfloat16),
            pltpu.VMEM((toks - rt, width), jnp.bfloat16),
            early_buf,
            early_buf,
            early_buf,
            late_buf,
            late_buf,
            late_buf,
            dma,
            dma((5,)),
            sems,
            sems,
            sems,
            sems,
            dma((8, 7)),
            dma((8, 7)),
        ],
        compiler_params=pltpu.CompilerParams(
            collective_id=1, has_side_effects=True, vmem_limit_bytes=VMEM_LIMIT
        ),
        name="chain",
    )(gated, piece, *near, extra)


def dup_body(x_ref, y_ref, x_out, y_out):
    x_out[...] = x_ref[...]
    y_out[...] = y_ref[...]


def dup(x, y):
    steps = 8
    specs = [pl.BlockSpec((a.shape[0] // steps, a.shape[1]), lambda i: (i, 0)) for a in (x, y)]
    return pl.pallas_call(
        dup_body,
        grid=(steps,),
        in_specs=specs,
        out_specs=specs,
        out_shape=[jax.ShapeDtypeStruct(a.shape, a.dtype) for a in (x, y)],
        cost_estimate=pl.CostEstimate(flops=0, bytes_accessed=4 * (x.size + y.size), transcendentals=0),
        name="dup",
    )(x, y)


def on_device(
    tokens, input_source, branch_source, output_source, gates_source, decay_param, block_order
):
    zs, fs = lax.axis_size("tensor"), lax.axis_size("fsdp")
    blocks = block_order.shape[0]
    per_dev = blocks // zs
    prompts = tokens.shape[0] // LEN
    picked = (block_order[:, None] == jnp.arange(blocks)[None, :]).astype(jnp.float32)
    soft = -8.0 * jax.nn.softplus(decay_param)
    own = lax.dynamic_slice_in_dim(picked, lax.axis_index("tensor") * per_dev, per_dev)
    rate = jnp.sum(own[:, :, None] * soft[None, :, :], axis=1)[:, None, :]
    sources = (input_source, branch_source, output_source)
    if fs == 8 and zs == 4:
        wi, wb, piece, extra, gates, branch_in, gate_pre = spread(
            block_order, sources, gates_source, tokens, zs, fs
        )
        near = [
            lax.ppermute(piece, "fsdp", [(f, peer(f)) for f in range(fs)])
            for peer in (
                lambda f: f + 2 - 4 * ((f // 2) % 2),
                lambda f: f + 4 - 8 * (f // 4),
                lambda f: f + 1 - 2 * (f % 2),
            )
        ]
        gated, wi, wb, gates = recur(branch_in, gate_pre, gates, rate, wi, wb, prompts)
        wo, mixed = chain(gated, piece, near, extra, zs, fs)
        wo, mixed = dup(wo, mixed)
        return mixed, wi, wb, wo, gates
    hot = picked.astype(jnp.bfloat16)
    sectioned = tuple(
        jnp.einsum(
            "jb,cbr->cjr", hot, s.astype(jnp.bfloat16), preferred_element_type=jnp.float32
        ).astype(jnp.bfloat16)
        for s in sources
    )
    gate_sectioned = jnp.einsum(
        "jb,gbio->gjio", hot, gates_source.astype(jnp.bfloat16), preferred_element_type=jnp.float32
    ).astype(jnp.bfloat16)
    gate_group = lax.all_to_all(gate_sectioned, "tensor", split_axis=1, concat_axis=3, tiled=True)
    gates = lax.all_gather(jnp.transpose(gate_group, (0, 1, 3, 2)), "fsdp", axis=3, tiled=True)
    regrouped = lax.all_to_all(sectioned, "tensor", split_axis=1, concat_axis=0, tiled=True)
    wi, wb, wo = (
        lax.all_gather(
            jnp.transpose(w, (2, 1, 0)).reshape(w.shape[2], -1), "fsdp", axis=0, tiled=True
        )
        for w in regrouped
    )
    branch_in = jnp.dot(tokens, wi, preferred_element_type=jnp.float32).astype(jnp.bfloat16)
    gate_pre = jnp.dot(tokens, wb, preferred_element_type=jnp.float32)
    gated, wi, wb, gates = recur(branch_in, gate_pre, gates, rate, wi, wb, prompts)
    partial_value = lax.dot_general(gated, wo, NT, preferred_element_type=jnp.float32)
    mixed = lax.psum_scatter(
        partial_value.astype(jnp.bfloat16), "tensor", scatter_dimension=1, tiled=True
    )
    return mixed, wi, wb, wo, gates


def solution(mesh):
    return jax.shard_map(
        on_device,
        mesh=mesh,
        in_specs=(
            P("fsdp", None),
            P("tensor", None, "fsdp"),
            P("tensor", None, "fsdp"),
            P("tensor", None, "fsdp"),
            P(None, None, "fsdp", "tensor"),
            P(),
            P(),
        ),
        out_specs=(
            P("fsdp", "tensor"),
            P(None, "tensor"),
            P(None, "tensor"),
            P(None, "tensor"),
            P(None, "tensor", None, None),
        ),
        check_vma=False,
    )
```

```python
import functools
import jax
import jax.numpy as jnp
from jax import lax
from jax.experimental import pallas as pl
from jax.experimental.pallas import tpu as pltpu
from jax.sharding import PartitionSpec as P

LEN = 256
SUB = 8
VMEM_LIMIT = 60 * 2**20
MESH = pl.DeviceIdType.MESH
NT = (((1,), (1,)), ((), ()))


def recur_body(
    prompts, x_ref, pre_ref, g_ref, r_ref, wi_ref, wb_ref,
    o_ref, wi_out, wb_out, g_out, a_s, d_s, carry,
):
    @pl.when(pl.program_id(1) == 0)
    def _():
        carry[...] = jnp.zeros_like(carry)
        g_out[...] = g_ref[...]

    wi_out[...] = wi_ref[...]
    wb_out[...] = wb_ref[...]
    x = x_ref[...]
    pre_r = lax.dot_general(x, g_ref[0, 0], NT, preferred_element_type=jnp.float32)
    pre_i = lax.dot_general(x, g_ref[1, 0], NT, preferred_element_type=jnp.float32)
    a = jnp.exp(r_ref[0] * jax.nn.sigmoid(pre_r))
    a_s[...] = a
    d_s[...] = jnp.sqrt(jnp.maximum(1.0 - a * a, 0.0)) * (
        jax.nn.sigmoid(pre_i) * x.astype(jnp.float32)
    )
    rows, chan = a_s.shape
    group = lax.broadcasted_iota(jnp.int32, (SUB, chan), 0) // prompts

    def last(v):
        res = v
        for g in range(SUB // prompts - 1):
            res = jnp.where(group == g, pltpu.roll(v, (g + 1) * prompts, 0), res)
        return res

    def step(i, c):
        at = pl.ds(pl.multiple_of(i * SUB, SUB), SUB)
        a = a_s[at, :]
        d = d_s[at, :]
        shift = 1
        while shift < SUB // prompts:
            a_sh = pltpu.roll(a, shift * prompts, 0)
            d_sh = pltpu.roll(d, shift * prompts, 0)
            d = jnp.where(group >= shift, a * d_sh + d, d)
            a = jnp.where(group >= shift, a * a_sh, a)
            shift *= 2
        d_s[at, :] = a * c + d
        return last(a) * c + last(d)

    carry[...] = lax.fori_loop(0, rows // SUB, step, carry[...], unroll=8)
    o_ref[...] = (d_s[...] * jax.nn.gelu(pre_ref[...], approximate=True)).astype(o_ref.dtype)


def recur(branch_in, gate_pre, gates, rate, wi, wb, prompts):
    rows, width = branch_in.shape
    blocks, chan = gates.shape[1], gates.shape[2]
    tile = min(rows, 256)
    tiles = rows // tile
    part = wi.shape[0] // (blocks * tiles)
    cell = pl.BlockSpec((tile, chan), lambda b, t: (t, b))
    gate = pl.BlockSpec((2, 1, chan, chan), lambda b, t: (0, b, 0, 0))
    slab = pl.BlockSpec((part, width), lambda b, t: (b * tiles + t, 0))
    return pl.pallas_call(
        functools.partial(recur_body, prompts),
        grid=(blocks, tiles),
        in_specs=[cell, cell, gate, pl.BlockSpec((1, 1, chan), lambda b, t: (b, 0, 0)), slab, slab],
        out_specs=[cell, slab, slab, gate],
        out_shape=[
            jax.ShapeDtypeStruct((rows, width), jnp.bfloat16),
            jax.ShapeDtypeStruct(wi.shape, wi.dtype),
            jax.ShapeDtypeStruct(wb.shape, wb.dtype),
            jax.ShapeDtypeStruct(gates.shape, gates.dtype),
        ],
        scratch_shapes=[
            pltpu.VMEM((tile, chan), jnp.float32),
            pltpu.VMEM((tile, chan), jnp.float32),
            pltpu.VMEM((SUB, chan), jnp.float32),
        ],
        compiler_params=pltpu.CompilerParams(
            dimension_semantics=("arbitrary", "arbitrary"), vmem_limit_bytes=VMEM_LIMIT
        ),
        cost_estimate=pl.CostEstimate(
            flops=4 * rows * width * chan, bytes_accessed=8 * rows * width, transcendentals=6 * rows * width
        ),
        name="recur",
    )(branch_in, gate_pre, gates, rate, wi, wb)


def places():
    f = lax.axis_index("fsdp")
    sib = f + 1 - 2 * (f % 2)
    xp = f + 2 - 4 * ((f // 2) % 2)
    yp = f + 4 - 8 * (f // 4)
    diag = xp + 4 - 8 * (xp // 4)
    return f, sib, xp, yp, diag


def greet(zs, z, peers):
    barrier = pltpu.get_barrier_semaphore()
    for peer in peers:
        pl.semaphore_signal(barrier, inc=1, device_id={"fsdp": peer}, device_id_type=MESH)
    for k in range(1, zs):
        pl.semaphore_signal(
            barrier, inc=1, device_id={"tensor": (z + k) % zs}, device_id_type=MESH
        )
    pl.semaphore_wait(barrier, len(peers) + zs - 1)


def gatherer(view, f_send, f_recv):
    f, sib, xp, yp, diag = places()

    def make(q, i):
        near, far = ((xp, yp), (yp, xp))[q % 2]
        owner, peer = (
            (f, xp), (f, yp), (f, sib), (near, far), (xp, sib), (yp, sib), (diag, sib),
        )[i]
        at = view(q, owner)
        return pltpu.make_async_remote_copy(
            src_ref=at,
            dst_ref=at,
            send_sem=f_send.at[q, i],
            recv_sem=f_recv.at[q, i],
            device_id={"fsdp": peer},
            device_id_type=MESH,
        )

    def first(q):
        for i in range(3):
            make(q, i).start()

    def relay(q):
        make(q, 0).wait_recv()
        if q % 2 == 0:
            make(q, 3).start()
        make(q, 4).start()
        make(q, 1).wait_recv()
        if q % 2 == 1:
            make(q, 3).start()
        make(q, 5).start()

    def across(q):
        make(q, 3).wait_recv()
        make(q, 6).start()

    def have(q, *ways):
        for i in ways:
            make(q, i).wait_recv()

    def hand(q):
        for i in (3, 4, 5):
            make(q, i).start()

    def drain(qs, ways=range(7)):
        for q in qs:
            for i in ways:
                make(q, i).wait_send()

    return first, relay, across, have, drain, hand


def spread_body(
    order, src0, src1, src2, gsrc, tokens,
    out0, out1, piece2, extra, gates_out, x_out, pre_out,
    perm, srcv, xb, sbuf, gsend, held, gheld, gfull, wfull, tok, acc, acc_pre, x_held, piece_v,
    src_sem, x_sem, pre_sem, piece_sem, tok_sem, own_sem, z_send, z_recv, e_send, e_recv, put_sem, f_send, f_recv,
):
    srcs = (src0, src1, src2)
    z = lax.axis_index("tensor")
    f, sib, xp, yp, diag = places()
    zs, per, chan = held.shape[2], held.shape[3], held.shape[4]
    rows = src0.shape[2]
    half = rows // 2
    ghalf = gheld.shape[3] // 2
    group = per * chan
    tok_copy = pltpu.make_async_copy(tokens, tok, tok_sem)
    src_copy = [pltpu.make_async_copy(srcs[w], srcv.at[w], src_sem.at[w]) for w in range(3)]
    src_copy[0].start()

    def cast(w):
        src_copy[w].wait()
        xb[...] = srcv[w].reshape(xb.shape).astype(jnp.bfloat16)
        for k in range(zs):
            part = jnp.dot(
                perm[k * group : (k + 1) * group, :], xb[...], preferred_element_type=jnp.float32
            )
            part = part.astype(jnp.bfloat16).reshape(per, chan, rows)
            for p in range(2):
                sbuf[w, p, k * per : (k + 1) * per] = part[:, :, p * half : (p + 1) * half]

    blocks = sbuf.shape[2]
    column = lax.broadcasted_iota(jnp.int32, (chan, perm.shape[1]), 1)
    channel = lax.broadcasted_iota(jnp.int32, (chan, perm.shape[1]), 0) * blocks
    for j in range(blocks):
        perm[j * chan : (j + 1) * chan, :] = jnp.where(
            column == channel + order[j], 1.0, 0.0
        ).astype(jnp.bfloat16)
    cast(0)
    src_copy[1].start()
    src_copy[2].start()
    tok_copy.start()
    greet(zs, z, (sib, xp, yp))

    def z_source(q, to):
        if q == 6:
            return gsend.at[:, pl.ds(to * per, per)]
        return sbuf.at[q // 2, q % 2, pl.ds(to * per, per)]

    def z_target(q):
        if q == 6:
            return gheld.at[z]
        return held.at[q // 2, q % 2, z]

    a2a, own = {}, {}
    queue = [0, 1, 2, 6, 3, 4, 5]

    def exchange(q, i, to, sender):
        return pltpu.make_async_remote_copy(
            src_ref=z_source(q, to),
            dst_ref=z_target(q),
            send_sem=z_send.at[q, i],
            recv_sem=z_recv.at[q, sender],
            device_id={"tensor": to},
            device_id_type=MESH,
        )

    def depart():
        q = queue.pop(0)
        for i in range(zs - 1):
            up = (z + i + 1) % zs
            down = zs - 1 - (zs - z + i) % zs
            to = jnp.where(z < zs // 2, up, down)
            a2a[q, i] = exchange(q, i, to, z)
            a2a[q, i].start()
        own[q] = pltpu.make_async_copy(z_source(q, z), z_target(q), own_sem.at[q])
        own[q].start()

    depart()
    cast(1)
    cast(2)
    for g in range(gsend.shape[0]):
        for j in range(gsend.shape[1]):
            gsend[g, j] = gsrc[g, order[j]].astype(jnp.bfloat16)

    def arrive(q):
        own[q].wait()
        for k in range(1, zs):
            other = (z + k) % zs
            exchange(q, 0, other, other).wait_recv()
        for _ in range(2 if q == 0 else 1):
            if queue:
                depart()

    def slab(q, b):
        return jnp.concatenate([held[q // 2, q % 2, s, b] for s in range(zs)], axis=0).T

    def view(q, owner):
        if q >= 4:
            return gfull.at[:, :, pl.ds(owner * 2 * ghalf + (q - 4) * ghalf, ghalf)]
        return wfull.at[q // 2, pl.ds(owner * rows + (q % 2) * half, half)]

    send_first, relay, across, have, drain, _ = gatherer(view, f_send, f_recv)

    def first(q):
        if q < 4:
            arrive(q)
            at = pl.ds(pl.multiple_of(f * rows + (q % 2) * half, half), half)
            for b in range(per):
                width = chan * zs
                wfull[q // 2, at, b * width : (b + 1) * width] = slab(q, b)
        send_first(q)

    def first_out(q):
        arrive(q)
        at = slice((q % 2) * half, (q % 2) * half + half)
        for b in range(per):
            width = chan * zs
            piece_v[at, b * width : (b + 1) * width] = slab(q, b)
        piece_copy(q).start()
        for end, inner in ((0, 1), (zs - 1, zs - 2)):
            @pl.when(z == end)
            def _():
                ahead(q, inner).start()

    def piece_copy(q):
        at = pl.ds((q % 2) * half, half)
        return pltpu.make_async_copy(piece_v.at[at], piece2.at[at], piece_sem.at[q % 2])

    def ahead(q, to):
        at = pl.ds((q % 2) * half, half)
        return pltpu.make_async_remote_copy(
            src_ref=piece_v.at[at],
            dst_ref=extra.at[at],
            send_sem=e_send.at[q % 2],
            recv_sem=e_recv.at[q % 2],
            device_id={"tensor": to},
            device_id_type=MESH,
        )

    put = []
    tile = 256
    deep = 2 * rows
    tiles = tok.shape[0] // tile

    def result(w, i):
        at = pl.ds(pl.multiple_of(i * tile, tile), tile)
        if w == 0:
            return pltpu.make_async_copy(x_held.at[at], x_out.at[at], x_sem.at[i])
        return pltpu.make_async_copy(acc_pre.at[at], pre_out.at[at], pre_sem.at[i])

    def product(w, part, mode):
        base = pl.multiple_of(part * deep, deep)
        outs = (out0, out1)
        copy = pltpu.make_async_copy(
            wfull.at[w, pl.ds(base, deep)], outs[w].at[pl.ds(base, deep)], put_sem.at[len(put)]
        )
        copy.start()
        put.append(copy)
        dst = (acc, acc_pre)[w]

        def step(i, c):
            at = pl.ds(pl.multiple_of(i * tile, tile), tile)
            value = jnp.dot(
                tok[at, pl.ds(base, deep)],
                wfull[w, pl.ds(base, deep), :],
                preferred_element_type=jnp.float32,
            )
            if mode != "first":
                value = value + dst[at, :]
            if w == 0 and mode == "last":
                x_held[at, :] = value.astype(jnp.bfloat16)
            else:
                dst[at, :] = value
            if mode == "last":
                result(w, i).start()
            return c

        lax.fori_loop(0, tiles, step, 0)

    chip, chip_x, chip_y, chip_d = f // 2, xp // 2, yp // 2, diag // 2

    first(0)
    first(1)
    relay(0)
    first(2)
    arrive(6)
    for h in range(2):
        for g in range(gfull.shape[0]):
            for b in range(per):
                at = pl.ds(pl.multiple_of((f * 2 + h) * ghalf, ghalf), ghalf)
                gfull[g, b, at, :] = jnp.concatenate(
                    [gheld[s, g, b, h * ghalf : (h + 1) * ghalf, :] for s in range(zs)], axis=1
                )
    first(4)
    first(5)
    relay(1)
    first(3)
    tok_copy.wait()
    have(0, 2)
    have(1, 2)
    product(0, chip, "first")
    across(0)
    relay(2)
    have(0, 4)
    have(1, 4)
    product(0, chip_x, "more")
    relay(4)
    relay(5)
    first_out(4)
    across(1)
    have(0, 5)
    have(1, 5)
    product(0, chip_y, "more")
    relay(3)
    have(0, 6)
    have(1, 6)
    product(0, chip_d, "last")
    first_out(5)
    for q in (4, 5, 2):
        across(q)
    have(2, 2)
    have(3, 2)
    product(1, chip, "first")
    have(2, 4)
    have(3, 4)
    product(1, chip_x, "more")
    across(3)
    have(2, 5)
    have(3, 5)
    product(1, chip_y, "more")
    for q in (4, 5):
        have(q, 2, 4, 5, 6)
    for g in range(gfull.shape[0]):
        for b in range(per):
            gates_out[g, b] = gfull[g, b].T
    have(2, 6)
    have(3, 6)
    product(1, chip_d, "last")
    for end, inner in ((0, 1), (zs - 1, zs - 2)):
        @pl.when(z == end)
        def _():
            for q in (4, 5):
                ahead(q, inner).wait_send()

        @pl.when(z == inner)
        def _():
            for q in (4, 5):
                ahead(q, end).wait_recv()

    for copy in put:
        copy.wait()
    for i in range(tiles):
        result(0, i).wait()
        result(1, i).wait()
    piece_copy(4).wait()
    piece_copy(5).wait()
    drain(range(6))
    for q in range(7):
        for i in range(zs - 1):
            a2a[q, i].wait_send()


def spread(order, sources, gates, tokens, zs, fs):
    chan, blocks, rows = sources[0].shape
    kinds, _, gin, gout = gates.shape
    per = blocks // zs
    width = per * chan * zs
    toks = tokens.shape[0]
    full = jax.ShapeDtypeStruct((rows * fs, width), jnp.bfloat16)
    vmem = pl.BlockSpec(memory_space=pltpu.VMEM)
    hbm = pl.BlockSpec(memory_space=pl.ANY)
    dma = pltpu.SemaphoreType.DMA
    return pl.pallas_call(
        spread_body,
        in_specs=[pl.BlockSpec(memory_space=pltpu.SMEM)] + [hbm] * 3 + [vmem, hbm],
        out_specs=[hbm, hbm, hbm, hbm, vmem, hbm, hbm],
        out_shape=[
            full,
            full,
            jax.ShapeDtypeStruct((rows, width), jnp.bfloat16),
            jax.ShapeDtypeStruct((rows, width), jnp.bfloat16),
            jax.ShapeDtypeStruct((kinds, per, gout * zs, gin * fs), jnp.bfloat16),
            jax.ShapeDtypeStruct((toks, width), jnp.bfloat16),
            jax.ShapeDtypeStruct((toks, width), jnp.float32),
        ],
        scratch_shapes=[
            pltpu.VMEM((chan * blocks, chan * blocks), jnp.bfloat16),
            pltpu.VMEM((3, chan, blocks, rows), jnp.float32),
            pltpu.VMEM((chan * blocks, rows), jnp.bfloat16),
            pltpu.VMEM((3, 2, blocks, chan, rows // 2), jnp.bfloat16),
            pltpu.VMEM((kinds, blocks, gin, gout), jnp.bfloat16),
            pltpu.VMEM((3, 2, zs, per, chan, rows // 2), jnp.bfloat16),
            pltpu.VMEM((zs, kinds, per, gin, gout), jnp.bfloat16),
            pltpu.VMEM((kinds, per, gin * fs, gout * zs), jnp.bfloat16),
            pltpu.VMEM((2, rows * fs, width), jnp.bfloat16),
            pltpu.VMEM(tokens.shape, jnp.bfloat16),
            pltpu.VMEM((toks, width), jnp.float32),
            pltpu.VMEM((toks, width), jnp.float32),
            pltpu.VMEM((toks, width), jnp.bfloat16),
            pltpu.VMEM((rows, width), jnp.bfloat16),
            dma((3,)),
            dma((toks // 256,)),
            dma((toks // 256,)),
            dma((2,)),
            dma,
            dma((7,)),
            dma((7, zs)),
            dma((7, zs)),
            dma((2,)),
            dma((2,)),
            dma((8,)),
            dma((6, 7)),
            dma((6, 7)),
        ],
        compiler_params=pltpu.CompilerParams(
            collective_id=0, has_side_effects=True, vmem_limit_bytes=VMEM_LIMIT
        ),
        name="spread",
    )(order, *sources, gates, tokens)


def chain_body(
    gated, piece, piece_x, piece_y, piece_s, extra, out, mixed,
    wfull, wend, rows_in, early_out, early_right, early_left, late_out, late_right, late_left,
    put_sem, get_sem, r_send, r_recv, l_send, l_recv, f_send, f_recv,
):
    z = lax.axis_index("tensor")
    zs = lax.axis_size("tensor")
    f, sib, xp, yp, diag = places()
    rows = piece.shape[0]
    parts = 4
    part = rows // parts
    cut, rt = early_out.shape[2], early_out.shape[1]
    wide, lt = late_out.shape[3], late_out.shape[2]
    cuts = wfull.shape[0] // cut
    quarter = cuts // zs
    halves = rows // cut
    late = (gated.shape[0] - rt) // lt
    inner = (z > 0) & (z < zs - 1)
    gets = []
    for ref, to, owner in (
        (piece_x, wfull, xp), (piece_y, wfull, yp), (piece, wfull, f), (piece_s, wfull, sib), (extra, wend, f),
    ):
        at = pl.ds(pl.multiple_of(owner * rows, rows), rows)
        gets.append(pltpu.make_async_copy(ref, to.at[at], get_sem.at[len(gets)]))
        gets[-1].start()
    greet(zs, z, (sib, xp, yp))

    def view(q, owner):
        to = wfull if q < parts else wend
        return to.at[pl.ds(owner * rows + (q % parts) * part, part)]

    first, relay, across, have, drain, hand = gatherer(view, f_send, f_recv)

    def dot(x, w, at):
        return lax.dot_general(x, w[at, :], NT, preferred_element_type=jnp.float32)

    def early_term(d):
        return dot(gated[:rt, :], wfull, pl.ds(d * cut, cut))

    def late_rows(t):
        return slice(rt + t * lt, rt + (t + 1) * lt)

    def late_term(t, q):
        return dot(gated[late_rows(t), :], wfull, pl.ds(q * wide, wide))

    def end_term(t, q):
        return dot(rows_in[t * lt : (t + 1) * lt, :], wend, pl.ds(q * wide, wide))

    def move(src, dst, s, forward):
        return pltpu.make_async_remote_copy(
            src_ref=src,
            dst_ref=dst,
            send_sem=(r_send if forward else l_send).at[s],
            recv_sem=(r_recv if forward else l_recv).at[s],
            device_id={"tensor": (z + (1 if forward else zs - 1)) % zs},
            device_id_type=MESH,
        )

    def early_move(d, forward):
        ins = early_right if forward else early_left
        return move(early_out.at[d], ins.at[d], d, forward)

    def late_move(t, q, forward):
        ins = late_right if forward else late_left
        return move(late_out.at[q, t], ins.at[q, t], cuts + q * late + t, forward)

    def row_move(t, forward):
        return move(
            gated.at[pl.ds(rt + t * lt, lt)], rows_in.at[pl.ds(t * lt, lt)],
            cuts + zs * late + t, forward,
        )

    def ordered(q):
        return sorted(range(q * quarter, (q + 1) * quarter), key=lambda d: (d % halves, d))

    lists, sends = {}, {}
    for forward in (True, False):
        far = range(zs - 1, 0, -1) if forward else range(zs - 1)
        groups = [[("early", d) for d in ordered(q)] for q in far]
        groups.insert(zs - 2, [("rows", t) for t in range(late)])
        lists[forward] = [item for group in groups for item in group]
        start = lists[forward].index(("rows", 0))
        sends[forward] = list(lists[forward])
        sends[forward].insert(0, sends[forward].pop(start))

    def one(forward, k):
        kind, n = sends[forward][k]
        return early_move(n, forward) if kind == "early" else row_move(n, forward)

    def early_pass(d, forward):
        value = early_term(d)
        early_move(d, forward).wait_recv()
        ins = early_right if forward else early_left
        early_out[d] = (value + ins[d].astype(jnp.float32)).astype(jnp.bfloat16)
        early_move(d, forward).start()

    def late_pass(t, q, forward):
        value = late_term(t, q)
        late_move(t, q, forward).wait_recv()
        ins = late_right if forward else late_left
        late_out[q, t] = (value + ins[q, t].astype(jnp.float32)).astype(jnp.bfloat16)
        late_move(t, q, forward).start()

    def end(forward, away):
        return z == (away if forward else zs - 1 - away)

    def beyond(forward, away):
        return range(zs - 1, away, -1) if forward else range(zs - 1 - away)

    def step(k):
        for forward in (True, False):
            given, m = sends[forward][k]

            @pl.when(end(forward, 0))
            def _():
                if given == "early":
                    early_out[m] = early_term(m).astype(jnp.bfloat16)
                if k >= 2:
                    one(forward, k - 2).wait_send()
                one(forward, k).start()

            kind, n = lists[forward][k]
            if kind == "rows":
                @pl.when(end(forward, 1))
                def _():
                    row_move(n, forward).wait_recv()
                    for q in beyond(forward, 1):
                        late_out[q, n] = (late_term(n, q) + end_term(n, q)).astype(jnp.bfloat16)
                        late_move(n, q, forward).start()

        for forward in (True, False):
            kind, n = lists[forward][k]
            for away in range(1, zs - 1):
                if kind == "early":
                    if n // quarter in beyond(forward, away):
                        @pl.when(end(forward, away))
                        def _():
                            early_pass(n, forward)
                elif away > 1:
                    @pl.when(end(forward, away))
                    def _():
                        for q in beyond(forward, away):
                            late_pass(n, q, forward)

    def all_of(q):
        have(q, 2, 4, 5, 6)

    def when_inner(*acts):
        @pl.when(inner)
        def _():
            for act, q in acts:
                act(q)

    def last_late(c, t):
        value = late_term(t, c)
        if c in (1, zs - 2):
            value = value + end_term(t, c)
        if c > 1:
            late_move(t, c, True).wait_recv()
            value = value + late_right[c, t].astype(jnp.float32)
        if c < zs - 2:
            late_move(t, c, False).wait_recv()
            value = value + late_left[c, t].astype(jnp.float32)
        mixed[late_rows(t), :] = value.astype(mixed.dtype)

    def last_early(c, d):
        value = early_term(d)
        if c < zs - 1:
            early_move(d, False).wait_recv()
            value = value + early_left[d].astype(jnp.float32)
        if c > 0:
            early_move(d, True).wait_recv()
            value = value + early_right[d].astype(jnp.float32)
        e = d - c * quarter
        mixed[:rt, e * cut : (e + 1) * cut] = value.astype(mixed.dtype)

    def on_each(cs, act):
        for c in cs:
            @pl.when(z == c)
            def _():
                act(c)

    for get in gets[:2]:
        get.wait()
    hand(0)
    hand(1)
    for get in gets[2:]:
        get.wait()
    across(0)
    across(1)
    hand(2)
    hand(3)
    when_inner((first, parts), (first, parts + 1))
    have(0, 4, 5, 6)
    have(1, 4, 5, 6)
    step(0)
    across(2)
    across(3)
    step(1)
    have(2, 4, 5, 6)
    have(3, 4, 5, 6)
    put = pltpu.make_async_copy(wfull, out, put_sem)
    put.start()
    when_inner((relay, parts), (relay, parts + 1), (first, parts + 2), (first, parts + 3))
    step(2)
    step(3)
    when_inner((across, parts), (across, parts + 1))
    step(4)
    when_inner((relay, parts + 2), (relay, parts + 3))
    step(5)
    step(6)
    when_inner((across, parts + 2), (across, parts + 3))
    step(7)
    when_inner(*((all_of, parts + q) for q in range(parts)))
    count = len(lists[True])
    ends = (0, zs - 1)
    for k in range(8, count):
        step(k)
        if k < 8 + quarter:
            on_each(ends, lambda c: last_early(c, ordered(c)[k - 8]))
        if k >= count - late:
            on_each(range(zs), lambda c: last_late(c, k - count + late))

    for c in range(zs):
        @pl.when(z == c)
        def _():
            if c not in ends:
                for d in ordered(c):
                    last_early(c, d)
            for forward in (True, False):
                away = c if forward else zs - 1 - c
                if away == 0:
                    for k in range(count - 2, count):
                        one(forward, k).wait_send()
                else:
                    for q in beyond(forward, away):
                        for d in ordered(q):
                            early_move(d, forward).wait_send()
                        for t in range(late):
                            late_move(t, q, forward).wait_send()

    drain(range(parts), range(3, 7))
    when_inner((drain, range(parts, 2 * parts)))
    put.wait()


def chain(gated, piece, near, extra, zs, fs):
    rows, width = piece.shape
    toks = gated.shape[0]
    depth = rows * fs
    cut, rt = rows // 2, toks // 2
    wide, lt = depth // zs, toks // 8
    late = (toks - rt) // lt
    vmem = pl.BlockSpec(memory_space=pltpu.VMEM)
    hbm = pl.BlockSpec(memory_space=pl.ANY)
    dma = pltpu.SemaphoreType.DMA
    early_buf = pltpu.VMEM((depth // cut, rt, cut), jnp.bfloat16)
    late_buf = pltpu.VMEM((zs, late, lt, wide), jnp.bfloat16)
    sems = dma((depth // cut + (zs + 1) * late,))
    return pl.pallas_call(
        chain_body,
        in_specs=[vmem] + [hbm] * 5,
        out_specs=[hbm, vmem],
        out_shape=[
            jax.ShapeDtypeStruct((depth, width), jnp.bfloat16),
            jax.ShapeDtypeStruct((toks, depth // zs), jnp.bfloat16),
        ],
        scratch_shapes=[
            pltpu.VMEM((depth, width), jnp.bfloat16),
            pltpu.VMEM((depth, width), jnp.bfloat16),
            pltpu.VMEM((toks - rt, width), jnp.bfloat16),
            early_buf,
            early_buf,
            early_buf,
            late_buf,
            late_buf,
            late_buf,
            dma,
            dma((5,)),
            sems,
            sems,
            sems,
            sems,
            dma((8, 7)),
            dma((8, 7)),
        ],
        compiler_params=pltpu.CompilerParams(
            collective_id=1, has_side_effects=True, vmem_limit_bytes=VMEM_LIMIT
        ),
        name="chain",
    )(gated, piece, *near, extra)


def dup_body(x_ref, y_ref, x_out, y_out):
    x_out[...] = x_ref[...]
    y_out[...] = y_ref[...]


def dup(x, y):
    steps = 8
    specs = [pl.BlockSpec((a.shape[0] // steps, a.shape[1]), lambda i: (i, 0)) for a in (x, y)]
    return pl.pallas_call(
        dup_body,
        grid=(steps,),
        in_specs=specs,
        out_specs=specs,
        out_shape=[jax.ShapeDtypeStruct(a.shape, a.dtype) for a in (x, y)],
        cost_estimate=pl.CostEstimate(flops=0, bytes_accessed=4 * (x.size + y.size), transcendentals=0),
        name="dup",
    )(x, y)


def on_device(
    tokens, input_source, branch_source, output_source, gates_source, decay_param, block_order
):
    zs, fs = lax.axis_size("tensor"), lax.axis_size("fsdp")
    blocks = block_order.shape[0]
    per_dev = blocks // zs
    prompts = tokens.shape[0] // LEN
    picked = (block_order[:, None] == jnp.arange(blocks)[None, :]).astype(jnp.float32)
    soft = -8.0 * jax.nn.softplus(decay_param)
    own = lax.dynamic_slice_in_dim(picked, lax.axis_index("tensor") * per_dev, per_dev)
    rate = jnp.sum(own[:, :, None] * soft[None, :, :], axis=1)[:, None, :]
    sources = (input_source, branch_source, output_source)
    if fs == 8 and zs == 4:
        wi, wb, piece, extra, gates, branch_in, gate_pre = spread(
            block_order, sources, gates_source, tokens, zs, fs
        )
        near = [
            lax.ppermute(piece, "fsdp", [(f, peer(f)) for f in range(fs)])
            for peer in (
                lambda f: f + 2 - 4 * ((f // 2) % 2),
                lambda f: f + 4 - 8 * (f // 4),
                lambda f: f + 1 - 2 * (f % 2),
            )
        ]
        gated, wi, wb, gates = recur(branch_in, gate_pre, gates, rate, wi, wb, prompts)
        wo, mixed = chain(gated, piece, near, extra, zs, fs)
        wo, mixed = dup(wo, mixed)
        return mixed, wi, wb, wo, gates
    hot = picked.astype(jnp.bfloat16)
    sectioned = tuple(
        jnp.einsum(
            "jb,cbr->cjr", hot, s.astype(jnp.bfloat16), preferred_element_type=jnp.float32
        ).astype(jnp.bfloat16)
        for s in sources
    )
    gate_sectioned = jnp.einsum(
        "jb,gbio->gjio", hot, gates_source.astype(jnp.bfloat16), preferred_element_type=jnp.float32
    ).astype(jnp.bfloat16)
    gate_group = lax.all_to_all(gate_sectioned, "tensor", split_axis=1, concat_axis=3, tiled=True)
    gates = lax.all_gather(jnp.transpose(gate_group, (0, 1, 3, 2)), "fsdp", axis=3, tiled=True)
    regrouped = lax.all_to_all(sectioned, "tensor", split_axis=1, concat_axis=0, tiled=True)
    wi, wb, wo = (
        lax.all_gather(
            jnp.transpose(w, (2, 1, 0)).reshape(w.shape[2], -1), "fsdp", axis=0, tiled=True
        )
        for w in regrouped
    )
    branch_in = jnp.dot(tokens, wi, preferred_element_type=jnp.float32).astype(jnp.bfloat16)
    gate_pre = jnp.dot(tokens, wb, preferred_element_type=jnp.float32)
    gated, wi, wb, gates = recur(branch_in, gate_pre, gates, rate, wi, wb, prompts)
    partial_value = lax.dot_general(gated, wo, NT, preferred_element_type=jnp.float32)
    mixed = lax.psum_scatter(
        partial_value.astype(jnp.bfloat16), "tensor", scatter_dimension=1, tiled=True
    )
    return mixed, wi, wb, wo, gates


def solution(mesh):
    return jax.shard_map(
        on_device,
        mesh=mesh,
        in_specs=(
            P("fsdp", None),
            P("tensor", None, "fsdp"),
            P("tensor", None, "fsdp"),
            P("tensor", None, "fsdp"),
            P(None, None, "fsdp", "tensor"),
            P(),
            P(),
        ),
        out_specs=(
            P("fsdp", "tensor"),
            P(None, "tensor"),
            P(None, "tensor"),
            P(None, "tensor"),
            P(None, "tensor", None, None),
        ),
        check_vma=False,
    )
```

```python
import functools
import jax
import jax.numpy as jnp
from jax import lax
from jax.experimental import pallas as pl
from jax.experimental.pallas import tpu as pltpu
from jax.sharding import PartitionSpec as P

LEN = 256
SUB = 8
VMEM_LIMIT = 60 * 2**20
MESH = pl.DeviceIdType.MESH
NT = (((1,), (1,)), ((), ()))


def recur_body(
    prompts, x_ref, pre_ref, g_ref, r_ref, wi_ref, wb_ref,
    o_ref, wi_out, wb_out, g_out, a_s, d_s, carry,
):
    @pl.when(pl.program_id(1) == 0)
    def _():
        carry[...] = jnp.zeros_like(carry)
        g_out[...] = g_ref[...]

    wi_out[...] = wi_ref[...]
    wb_out[...] = wb_ref[...]
    x = x_ref[...]
    pre_r = lax.dot_general(x, g_ref[0, 0], NT, preferred_element_type=jnp.float32)
    pre_i = lax.dot_general(x, g_ref[1, 0], NT, preferred_element_type=jnp.float32)
    a = jnp.exp(r_ref[0] * jax.nn.sigmoid(pre_r))
    a_s[...] = a
    d_s[...] = jnp.sqrt(jnp.maximum(1.0 - a * a, 0.0)) * (
        jax.nn.sigmoid(pre_i) * x.astype(jnp.float32)
    )
    rows, chan = a_s.shape
    group = lax.broadcasted_iota(jnp.int32, (SUB, chan), 0) // prompts

    def last(v):
        res = v
        for g in range(SUB // prompts - 1):
            res = jnp.where(group == g, pltpu.roll(v, (g + 1) * prompts, 0), res)
        return res

    def step(i, c):
        at = pl.ds(pl.multiple_of(i * SUB, SUB), SUB)
        a = a_s[at, :]
        d = d_s[at, :]
        shift = 1
        while shift < SUB // prompts:
            a_sh = pltpu.roll(a, shift * prompts, 0)
            d_sh = pltpu.roll(d, shift * prompts, 0)
            d = jnp.where(group >= shift, a * d_sh + d, d)
            a = jnp.where(group >= shift, a * a_sh, a)
            shift *= 2
        d_s[at, :] = a * c + d
        return last(a) * c + last(d)

    carry[...] = lax.fori_loop(0, rows // SUB, step, carry[...], unroll=8)
    o_ref[...] = (d_s[...] * jax.nn.gelu(pre_ref[...], approximate=True)).astype(o_ref.dtype)


def recur(branch_in, gate_pre, gates, rate, wi, wb, prompts):
    rows, width = branch_in.shape
    blocks, chan = gates.shape[1], gates.shape[2]
    tile = min(rows, 256)
    tiles = rows // tile
    part = wi.shape[0] // (blocks * tiles)
    cell = pl.BlockSpec((tile, chan), lambda b, t: (t, b))
    gate = pl.BlockSpec((2, 1, chan, chan), lambda b, t: (0, b, 0, 0))
    slab = pl.BlockSpec((part, width), lambda b, t: (b * tiles + t, 0))
    return pl.pallas_call(
        functools.partial(recur_body, prompts),
        grid=(blocks, tiles),
        in_specs=[cell, cell, gate, pl.BlockSpec((1, 1, chan), lambda b, t: (b, 0, 0)), slab, slab],
        out_specs=[cell, slab, slab, gate],
        out_shape=[
            jax.ShapeDtypeStruct((rows, width), jnp.bfloat16),
            jax.ShapeDtypeStruct(wi.shape, wi.dtype),
            jax.ShapeDtypeStruct(wb.shape, wb.dtype),
            jax.ShapeDtypeStruct(gates.shape, gates.dtype),
        ],
        scratch_shapes=[
            pltpu.VMEM((tile, chan), jnp.float32),
            pltpu.VMEM((tile, chan), jnp.float32),
            pltpu.VMEM((SUB, chan), jnp.float32),
        ],
        compiler_params=pltpu.CompilerParams(
            dimension_semantics=("arbitrary", "arbitrary"), vmem_limit_bytes=VMEM_LIMIT
        ),
        cost_estimate=pl.CostEstimate(
            flops=4 * rows * width * chan, bytes_accessed=8 * rows * width, transcendentals=6 * rows * width
        ),
        name="recur",
    )(branch_in, gate_pre, gates, rate, wi, wb)


def places():
    f = lax.axis_index("fsdp")
    sib = f + 1 - 2 * (f % 2)
    xp = f + 2 - 4 * ((f // 2) % 2)
    yp = f + 4 - 8 * (f // 4)
    diag = xp + 4 - 8 * (xp // 4)
    return f, sib, xp, yp, diag


def greet(zs, z, peers):
    barrier = pltpu.get_barrier_semaphore()
    for peer in peers:
        pl.semaphore_signal(barrier, inc=1, device_id={"fsdp": peer}, device_id_type=MESH)
    for k in range(1, zs):
        pl.semaphore_signal(
            barrier, inc=1, device_id={"tensor": (z + k) % zs}, device_id_type=MESH
        )
    pl.semaphore_wait(barrier, len(peers) + zs - 1)


def gatherer(view, f_send, f_recv):
    f, sib, xp, yp, diag = places()

    def make(q, i):
        near, far = ((xp, yp), (yp, xp))[q % 2]
        owner, peer = (
            (f, xp), (f, yp), (f, sib), (near, far), (xp, sib), (yp, sib), (diag, sib),
        )[i]
        at = view(q, owner)
        return pltpu.make_async_remote_copy(
            src_ref=at,
            dst_ref=at,
            send_sem=f_send.at[q, i],
            recv_sem=f_recv.at[q, i],
            device_id={"fsdp": peer},
            device_id_type=MESH,
        )

    def first(q):
        for i in range(3):
            make(q, i).start()

    def relay(q):
        make(q, 0).wait_recv()
        if q % 2 == 0:
            make(q, 3).start()
        make(q, 4).start()
        make(q, 1).wait_recv()
        if q % 2 == 1:
            make(q, 3).start()
        make(q, 5).start()

    def across(q):
        make(q, 3).wait_recv()
        make(q, 6).start()

    def have(q, *ways):
        for i in ways:
            make(q, i).wait_recv()

    def hand(q):
        for i in (3, 4, 5):
            make(q, i).start()

    def drain(qs, ways=range(7)):
        for q in qs:
            for i in ways:
                make(q, i).wait_send()

    return first, relay, across, have, drain, hand


def spread_body(
    order, src0, src1, src2, gsrc, tokens,
    out0, out1, piece2, gates_out, x_out, pre_out,
    perm, srcv, xb, sbuf, gsend, held, gheld, gfull, wfull, tok, acc, acc_pre, x_held, piece_v,
    src_sem, x_sem, pre_sem, piece_sem, tok_sem, own_sem, z_send, z_recv, put_sem, f_send, f_recv,
):
    srcs = (src0, src1, src2)
    z = lax.axis_index("tensor")
    f, sib, xp, yp, diag = places()
    zs, per, chan = held.shape[2], held.shape[3], held.shape[4]
    rows = src0.shape[2]
    half = rows // 2
    ghalf = gheld.shape[3] // 2
    group = per * chan
    tok_copy = pltpu.make_async_copy(tokens, tok, tok_sem)
    src_copy = [pltpu.make_async_copy(srcs[w], srcv.at[w], src_sem.at[w]) for w in range(3)]
    src_copy[0].start()

    def cast(w):
        src_copy[w].wait()
        xb[...] = srcv[w].reshape(xb.shape).astype(jnp.bfloat16)
        for k in range(zs):
            part = jnp.dot(
                perm[k * group : (k + 1) * group, :], xb[...], preferred_element_type=jnp.float32
            )
            part = part.astype(jnp.bfloat16).reshape(per, chan, rows)
            for p in range(2):
                sbuf[w, p, k * per : (k + 1) * per] = part[:, :, p * half : (p + 1) * half]

    blocks = sbuf.shape[2]
    column = lax.broadcasted_iota(jnp.int32, (chan, perm.shape[1]), 1)
    channel = lax.broadcasted_iota(jnp.int32, (chan, perm.shape[1]), 0) * blocks
    for j in range(blocks):
        perm[j * chan : (j + 1) * chan, :] = jnp.where(
            column == channel + order[j], 1.0, 0.0
        ).astype(jnp.bfloat16)
    cast(0)
    src_copy[1].start()
    src_copy[2].start()
    tok_copy.start()
    greet(zs, z, (sib, xp, yp))

    def z_source(q, to):
        if q == 6:
            return gsend.at[:, pl.ds(to * per, per)]
        return sbuf.at[q // 2, q % 2, pl.ds(to * per, per)]

    def z_target(q):
        if q == 6:
            return gheld.at[z]
        return held.at[q // 2, q % 2, z]

    a2a, own = {}, {}
    queue = [0, 1, 2, 6, 3, 4, 5]

    def exchange(q, i, to, sender):
        return pltpu.make_async_remote_copy(
            src_ref=z_source(q, to),
            dst_ref=z_target(q),
            send_sem=z_send.at[q, i],
            recv_sem=z_recv.at[q, sender],
            device_id={"tensor": to},
            device_id_type=MESH,
        )

    def depart():
        q = queue.pop(0)
        for i in range(zs - 1):
            up = (z + i + 1) % zs
            down = zs - 1 - (zs - z + i) % zs
            to = jnp.where(z < zs // 2, up, down)
            a2a[q, i] = exchange(q, i, to, z)
            a2a[q, i].start()
        own[q] = pltpu.make_async_copy(z_source(q, z), z_target(q), own_sem.at[q])
        own[q].start()

    depart()
    cast(1)
    cast(2)
    for g in range(gsend.shape[0]):
        for j in range(gsend.shape[1]):
            gsend[g, j] = gsrc[g, order[j]].astype(jnp.bfloat16)

    def arrive(q):
        own[q].wait()
        for k in range(1, zs):
            other = (z + k) % zs
            exchange(q, 0, other, other).wait_recv()
        for _ in range(2 if q == 0 else 1):
            if queue:
                depart()

    def slab(q, b):
        return jnp.concatenate([held[q // 2, q % 2, s, b] for s in range(zs)], axis=0).T

    def view(q, owner):
        if q >= 4:
            return gfull.at[:, :, pl.ds(owner * 2 * ghalf + (q - 4) * ghalf, ghalf)]
        return wfull.at[q // 2, pl.ds(owner * rows + (q % 2) * half, half)]

    send_first, relay, across, have, drain, _ = gatherer(view, f_send, f_recv)

    def first(q):
        if q < 4:
            arrive(q)
            at = pl.ds(pl.multiple_of(f * rows + (q % 2) * half, half), half)
            for b in range(per):
                width = chan * zs
                wfull[q // 2, at, b * width : (b + 1) * width] = slab(q, b)
        send_first(q)

    def first_out(q):
        arrive(q)
        at = slice((q % 2) * half, (q % 2) * half + half)
        for b in range(per):
            width = chan * zs
            piece_v[at, b * width : (b + 1) * width] = slab(q, b)
        piece_copy(q).start()

    def piece_copy(q):
        at = pl.ds((q % 2) * half, half)
        return pltpu.make_async_copy(piece_v.at[at], piece2.at[at], piece_sem.at[q % 2])

    put = []
    tile = 256
    deep = 2 * rows
    tiles = tok.shape[0] // tile

    def result(w, i):
        at = pl.ds(pl.multiple_of(i * tile, tile), tile)
        if w == 0:
            return pltpu.make_async_copy(x_held.at[at], x_out.at[at], x_sem.at[i])
        return pltpu.make_async_copy(acc_pre.at[at], pre_out.at[at], pre_sem.at[i])

    def product(w, part, mode):
        base = pl.multiple_of(part * deep, deep)
        outs = (out0, out1)
        copy = pltpu.make_async_copy(
            wfull.at[w, pl.ds(base, deep)], outs[w].at[pl.ds(base, deep)], put_sem.at[len(put)]
        )
        copy.start()
        put.append(copy)
        dst = (acc, acc_pre)[w]

        def step(i, c):
            at = pl.ds(pl.multiple_of(i * tile, tile), tile)
            value = jnp.dot(
                tok[at, pl.ds(base, deep)],
                wfull[w, pl.ds(base, deep), :],
                preferred_element_type=jnp.float32,
            )
            if mode != "first":
                value = value + dst[at, :]
            if w == 0 and mode == "last":
                x_held[at, :] = value.astype(jnp.bfloat16)
            else:
                dst[at, :] = value
            if mode == "last":
                result(w, i).start()
            return c

        lax.fori_loop(0, tiles, step, 0)

    chip, chip_x, chip_y, chip_d = f // 2, xp // 2, yp // 2, diag // 2

    first(0)
    first(1)
    relay(0)
    first(2)
    arrive(6)
    for h in range(2):
        for g in range(gfull.shape[0]):
            for b in range(per):
                at = pl.ds(pl.multiple_of((f * 2 + h) * ghalf, ghalf), ghalf)
                gfull[g, b, at, :] = jnp.concatenate(
                    [gheld[s, g, b, h * ghalf : (h + 1) * ghalf, :] for s in range(zs)], axis=1
                )
    first(4)
    first(5)
    relay(1)
    first(3)
    tok_copy.wait()
    have(0, 2)
    have(1, 2)
    product(0, chip, "first")
    across(0)
    relay(2)
    have(0, 4)
    have(1, 4)
    product(0, chip_x, "more")
    relay(4)
    relay(5)
    first_out(4)
    across(1)
    have(0, 5)
    have(1, 5)
    product(0, chip_y, "more")
    relay(3)
    have(0, 6)
    have(1, 6)
    product(0, chip_d, "last")
    first_out(5)
    for q in (4, 5, 2):
        across(q)
    have(2, 2)
    have(3, 2)
    product(1, chip, "first")
    have(2, 4)
    have(3, 4)
    product(1, chip_x, "more")
    across(3)
    have(2, 5)
    have(3, 5)
    product(1, chip_y, "more")
    for q in (4, 5):
        have(q, 2, 4, 5, 6)
    for g in range(gfull.shape[0]):
        for b in range(per):
            gates_out[g, b] = gfull[g, b].T
    have(2, 6)
    have(3, 6)
    product(1, chip_d, "last")
    for copy in put:
        copy.wait()
    for i in range(tiles):
        result(0, i).wait()
        result(1, i).wait()
    piece_copy(4).wait()
    piece_copy(5).wait()
    drain(range(6))
    for q in range(7):
        for i in range(zs - 1):
            a2a[q, i].wait_send()


def spread(order, sources, gates, tokens, zs, fs):
    chan, blocks, rows = sources[0].shape
    kinds, _, gin, gout = gates.shape
    per = blocks // zs
    width = per * chan * zs
    toks = tokens.shape[0]
    full = jax.ShapeDtypeStruct((rows * fs, width), jnp.bfloat16)
    vmem = pl.BlockSpec(memory_space=pltpu.VMEM)
    hbm = pl.BlockSpec(memory_space=pl.ANY)
    dma = pltpu.SemaphoreType.DMA
    return pl.pallas_call(
        spread_body,
        in_specs=[pl.BlockSpec(memory_space=pltpu.SMEM)] + [hbm] * 3 + [vmem, hbm],
        out_specs=[hbm, hbm, hbm, vmem, hbm, hbm],
        out_shape=[
            full,
            full,
            jax.ShapeDtypeStruct((rows, width), jnp.bfloat16),
            jax.ShapeDtypeStruct((kinds, per, gout * zs, gin * fs), jnp.bfloat16),
            jax.ShapeDtypeStruct((toks, width), jnp.bfloat16),
            jax.ShapeDtypeStruct((toks, width), jnp.float32),
        ],
        scratch_shapes=[
            pltpu.VMEM((chan * blocks, chan * blocks), jnp.bfloat16),
            pltpu.VMEM((3, chan, blocks, rows), jnp.float32),
            pltpu.VMEM((chan * blocks, rows), jnp.bfloat16),
            pltpu.VMEM((3, 2, blocks, chan, rows // 2), jnp.bfloat16),
            pltpu.VMEM((kinds, blocks, gin, gout), jnp.bfloat16),
            pltpu.VMEM((3, 2, zs, per, chan, rows // 2), jnp.bfloat16),
            pltpu.VMEM((zs, kinds, per, gin, gout), jnp.bfloat16),
            pltpu.VMEM((kinds, per, gin * fs, gout * zs), jnp.bfloat16),
            pltpu.VMEM((2, rows * fs, width), jnp.bfloat16),
            pltpu.VMEM(tokens.shape, jnp.bfloat16),
            pltpu.VMEM((toks, width), jnp.float32),
            pltpu.VMEM((toks, width), jnp.float32),
            pltpu.VMEM((toks, width), jnp.bfloat16),
            pltpu.VMEM((rows, width), jnp.bfloat16),
            dma((3,)),
            dma((toks // 256,)),
            dma((toks // 256,)),
            dma((2,)),
            dma,
            dma((7,)),
            dma((7, zs)),
            dma((7, zs)),
            dma((8,)),
            dma((6, 7)),
            dma((6, 7)),
        ],
        compiler_params=pltpu.CompilerParams(
            collective_id=0, has_side_effects=True, vmem_limit_bytes=VMEM_LIMIT
        ),
        name="spread",
    )(order, *sources, gates, tokens)


def chain_body(
    gated, piece, piece_x, piece_y, piece_s, extra, out, mixed,
    wfull, wend, rows_in, early_out, early_right, early_left, late_out, late_right, late_left,
    put_sem, get_sem, r_send, r_recv, l_send, l_recv, f_send, f_recv,
):
    z = lax.axis_index("tensor")
    zs = lax.axis_size("tensor")
    f, sib, xp, yp, diag = places()
    rows = piece.shape[0]
    parts = 4
    part = rows // parts
    cut, rt = early_out.shape[2], early_out.shape[1]
    wide, lt = late_out.shape[3], late_out.shape[2]
    cuts = wfull.shape[0] // cut
    quarter = cuts // zs
    halves = rows // cut
    late = (gated.shape[0] - rt) // lt
    pair = 2
    inner = (z > 0) & (z < zs - 1)
    gets = []
    for ref, to, owner in (
        (piece_x, wfull, xp), (piece_y, wfull, yp), (piece, wfull, f), (piece_s, wfull, sib), (extra, wend, f),
    ):
        at = pl.ds(pl.multiple_of(owner * rows, rows), rows)
        gets.append(pltpu.make_async_copy(ref, to.at[at], get_sem.at[len(gets)]))
        gets[-1].start()
    greet(zs, z, (sib, xp, yp))

    def view(q, owner):
        to = wfull if q < parts else wend
        return to.at[pl.ds(owner * rows + (q % parts) * part, part)]

    first, relay, across, have, drain, hand = gatherer(view, f_send, f_recv)

    def dot(x, w, at):
        return lax.dot_general(x, w[at, :], NT, preferred_element_type=jnp.float32)

    def early_term(d):
        return dot(gated[:rt, :], wfull, pl.ds(d * cut, cut))

    def late_rows(t):
        return slice(rt + t * lt, rt + (t + 1) * lt)

    def late_term(t, q):
        return dot(gated[late_rows(t), :], wfull, pl.ds(q * wide, wide))

    def end_term(t, q):
        return dot(rows_in[t * lt : (t + 1) * lt, :], wend, pl.ds(q * wide, wide))

    def move(src, dst, s, forward):
        return pltpu.make_async_remote_copy(
            src_ref=src,
            dst_ref=dst,
            send_sem=(r_send if forward else l_send).at[s],
            recv_sem=(r_recv if forward else l_recv).at[s],
            device_id={"tensor": (z + (1 if forward else zs - 1)) % zs},
            device_id_type=MESH,
        )

    def early_move(d, forward):
        ins = early_right if forward else early_left
        return move(early_out.at[d], ins.at[d], d, forward)

    def late_move(t, q, forward):
        ins = late_right if forward else late_left
        return move(late_out.at[q, t], ins.at[q, t], cuts + q * late + t, forward)

    def row_move(t, forward):
        return move(
            gated.at[pl.ds(rt + t * lt // pair, lt // pair)], rows_in.at[pl.ds(t * lt // pair, lt // pair)],
            cuts + zs * late + t, forward,
        )

    def ordered(q):
        return sorted(range(q * quarter, (q + 1) * quarter), key=lambda d: (d % halves, d))

    lists, sends = {}, {}
    for forward in (True, False):
        far = range(zs - 1, 0, -1) if forward else range(zs - 1)
        groups = [[("early", d) for d in ordered(q)] for q in far]
        lists[forward] = [item for group in groups for item in group]
        at = (zs - 2) * quarter
        lists[forward][at:at] = [("rows", t) for t in range(pair, pair * late)]
        lists[forward][at - 1 : at - 1] = [("rows", t) for t in range(pair)]
        sends[forward] = list(lists[forward])
        sends[forward].insert(0, sends[forward].pop(at - 1))

    def one(forward, k):
        kind, n = sends[forward][k]
        return early_move(n, forward) if kind == "early" else row_move(n, forward)

    def early_pass(d, forward):
        value = early_term(d)
        early_move(d, forward).wait_recv()
        ins = early_right if forward else early_left
        early_out[d] = (value + ins[d].astype(jnp.float32)).astype(jnp.bfloat16)
        early_move(d, forward).start()

    def late_pass(t, q, forward):
        value = late_term(t, q)
        late_move(t, q, forward).wait_recv()
        ins = late_right if forward else late_left
        late_out[q, t] = (value + ins[q, t].astype(jnp.float32)).astype(jnp.bfloat16)
        late_move(t, q, forward).start()

    def end(forward, away):
        return z == (away if forward else zs - 1 - away)

    def beyond(forward, away):
        return range(zs - 1, away, -1) if forward else range(zs - 1 - away)

    def step(k):
        for forward in (True, False):
            if k + 1 < len(sends[forward]):
                given, m = sends[forward][k + 1]

                @pl.when(end(forward, 0))
                def _():
                    if given == "early":
                        early_out[m] = early_term(m).astype(jnp.bfloat16)
                    if k >= 1:
                        one(forward, k - 1).wait_send()
                    one(forward, k + 1).start()

            kind, n = lists[forward][k]
            if kind == "rows":
                @pl.when(end(forward, 1))
                def _():
                    if n % pair < pair - 1:
                        row_move(n, forward).wait_recv()
                        return
                    t = n // pair
                    values = [late_term(t, q) for q in beyond(forward, 1)]
                    row_move(n, forward).wait_recv()
                    for q, value in zip(beyond(forward, 1), values):
                        late_out[q, t] = (value + end_term(t, q)).astype(jnp.bfloat16)
                        late_move(t, q, forward).start()

        for forward in (True, False):
            kind, n = lists[forward][k]
            for away in range(1, zs - 1):
                if kind == "early":
                    if n // quarter in beyond(forward, away):
                        @pl.when(end(forward, away))
                        def _():
                            early_pass(n, forward)
                elif away > 1 and n % pair == pair - 1:
                    @pl.when(end(forward, away))
                    def _():
                        for q in beyond(forward, away):
                            late_pass(n // pair, q, forward)

    def all_of(q):
        have(q, 2, 4, 5, 6)

    def when_inner(*acts):
        @pl.when(inner)
        def _():
            for act, q in acts:
                act(q)

    def last_late(c, t):
        value = late_term(t, c)
        if c in (1, zs - 2):
            value = value + end_term(t, c)
        if c > 1:
            late_move(t, c, True).wait_recv()
            value = value + late_right[c, t].astype(jnp.float32)
        if c < zs - 2:
            late_move(t, c, False).wait_recv()
            value = value + late_left[c, t].astype(jnp.float32)
        mixed[late_rows(t), :] = value.astype(mixed.dtype)

    def last_early(c, d):
        value = early_term(d)
        if c < zs - 1:
            early_move(d, False).wait_recv()
            value = value + early_left[d].astype(jnp.float32)
        if c > 0:
            early_move(d, True).wait_recv()
            value = value + early_right[d].astype(jnp.float32)
        e = d - c * quarter
        mixed[:rt, e * cut : (e + 1) * cut] = value.astype(mixed.dtype)

    def on_each(cs, act):
        for c in cs:
            @pl.when(z == c)
            def _():
                act(c)

    for forward in (True, False):
        @pl.when(end(forward, 0))
        def _():
            one(forward, 0).start()

    for get in gets[:2]:
        get.wait()
    hand(0)
    hand(1)
    for get in gets[2:]:
        get.wait()
    across(0)
    across(1)
    hand(2)
    hand(3)
    when_inner((first, parts), (first, parts + 1))
    have(0, 4, 5, 6)
    have(1, 4, 5, 6)
    step(0)
    across(2)
    across(3)
    step(1)
    have(2, 4, 5, 6)
    have(3, 4, 5, 6)
    put = pltpu.make_async_copy(wfull, out, put_sem)
    put.start()
    when_inner((relay, parts), (relay, parts + 1), (first, parts + 2), (first, parts + 3))
    step(2)
    step(3)
    when_inner((across, parts), (across, parts + 1))
    step(4)
    when_inner((relay, parts + 2), (relay, parts + 3))
    step(5)
    step(6)
    when_inner((across, parts + 2), (across, parts + 3))
    step(7)
    when_inner(*((all_of, parts + q) for q in range(parts)))
    count = len(lists[True])
    ends = (0, zs - 1)
    for k in range(8, count):
        step(k)
        if k < 8 + quarter:
            on_each(ends, lambda c: last_early(c, ordered(c)[k - 8]))
        if (count - 1 - k) % 2 == 0 and k > count - 1 - 2 * late:
            on_each(range(zs), lambda c: last_late(c, late - 1 - (count - 1 - k) // 2))

    for c in range(zs):
        @pl.when(z == c)
        def _():
            if c not in ends:
                for d in ordered(c):
                    last_early(c, d)
            for forward in (True, False):
                away = c if forward else zs - 1 - c
                if away == 0:
                    for k in range(count - 2, count):
                        one(forward, k).wait_send()
                else:
                    for q in beyond(forward, away):
                        for d in ordered(q):
                            early_move(d, forward).wait_send()
                        for t in range(late):
                            late_move(t, q, forward).wait_send()

    drain(range(parts), range(3, 7))
    when_inner((drain, range(parts, 2 * parts)))
    put.wait()


def chain(gated, piece, near, extra, zs, fs):
    rows, width = piece.shape
    toks = gated.shape[0]
    depth = rows * fs
    cut, rt = rows // 2, toks // 2
    wide, lt = depth // zs, toks // 4
    late = (toks - rt) // lt
    vmem = pl.BlockSpec(memory_space=pltpu.VMEM)
    hbm = pl.BlockSpec(memory_space=pl.ANY)
    dma = pltpu.SemaphoreType.DMA
    early_buf = pltpu.VMEM((depth // cut, rt, cut), jnp.bfloat16)
    late_buf = pltpu.VMEM((zs, late, lt, wide), jnp.bfloat16)
    sems = dma((depth // cut + (zs + 2) * late,))
    return pl.pallas_call(
        chain_body,
        in_specs=[vmem] + [hbm] * 5,
        out_specs=[hbm, vmem],
        out_shape=[
            jax.ShapeDtypeStruct((depth, width), jnp.bfloat16),
            jax.ShapeDtypeStruct((toks, depth // zs), jnp.bfloat16),
        ],
        scratch_shapes=[
            pltpu.VMEM((depth, width), jnp.bfloat16),
            pltpu.VMEM((depth, width), jnp.bfloat16),
            pltpu.VMEM((toks - rt, width), jnp.bfloat16),
            early_buf,
            early_buf,
            early_buf,
            late_buf,
            late_buf,
            late_buf,
            dma,
            dma((5,)),
            sems,
            sems,
            sems,
            sems,
            dma((8, 7)),
            dma((8, 7)),
        ],
        compiler_params=pltpu.CompilerParams(
            collective_id=1, has_side_effects=True, vmem_limit_bytes=VMEM_LIMIT
        ),
        name="chain",
    )(gated, piece, *near, extra)


def dup_body(x_ref, y_ref, x_out, y_out):
    x_out[...] = x_ref[...]
    y_out[...] = y_ref[...]


def dup(x, y):
    steps = 8
    specs = [pl.BlockSpec((a.shape[0] // steps, a.shape[1]), lambda i: (i, 0)) for a in (x, y)]
    return pl.pallas_call(
        dup_body,
        grid=(steps,),
        in_specs=specs,
        out_specs=specs,
        out_shape=[jax.ShapeDtypeStruct(a.shape, a.dtype) for a in (x, y)],
        cost_estimate=pl.CostEstimate(flops=0, bytes_accessed=4 * (x.size + y.size), transcendentals=0),
        name="dup",
    )(x, y)


def on_device(
    tokens, input_source, branch_source, output_source, gates_source, decay_param, block_order
):
    zs, fs = lax.axis_size("tensor"), lax.axis_size("fsdp")
    blocks = block_order.shape[0]
    per_dev = blocks // zs
    prompts = tokens.shape[0] // LEN
    picked = (block_order[:, None] == jnp.arange(blocks)[None, :]).astype(jnp.float32)
    soft = -8.0 * jax.nn.softplus(decay_param)
    own = lax.dynamic_slice_in_dim(picked, lax.axis_index("tensor") * per_dev, per_dev)
    rate = jnp.sum(own[:, :, None] * soft[None, :, :], axis=1)[:, None, :]
    sources = (input_source, branch_source, output_source)
    if fs == 8 and zs == 4:
        wi, wb, piece, gates, branch_in, gate_pre = spread(
            block_order, sources, gates_source, tokens, zs, fs
        )
        near = [
            lax.ppermute(piece, "fsdp", [(f, peer(f)) for f in range(fs)])
            for peer in (
                lambda f: f + 2 - 4 * ((f // 2) % 2),
                lambda f: f + 4 - 8 * (f // 4),
                lambda f: f + 1 - 2 * (f % 2),
            )
        ]
        extra = lax.ppermute(piece, "tensor", [(0, 1), (zs - 1, zs - 2)])
        gated, wi, wb, gates = recur(branch_in, gate_pre, gates, rate, wi, wb, prompts)
        wo, mixed = chain(gated, piece, near, extra, zs, fs)
        wo, mixed = dup(wo, mixed)
        return mixed, wi, wb, wo, gates
    hot = picked.astype(jnp.bfloat16)
    sectioned = tuple(
        jnp.einsum(
            "jb,cbr->cjr", hot, s.astype(jnp.bfloat16), preferred_element_type=jnp.float32
        ).astype(jnp.bfloat16)
        for s in sources
    )
    gate_sectioned = jnp.einsum(
        "jb,gbio->gjio", hot, gates_source.astype(jnp.bfloat16), preferred_element_type=jnp.float32
    ).astype(jnp.bfloat16)
    gate_group = lax.all_to_all(gate_sectioned, "tensor", split_axis=1, concat_axis=3, tiled=True)
    gates = lax.all_gather(jnp.transpose(gate_group, (0, 1, 3, 2)), "fsdp", axis=3, tiled=True)
    regrouped = lax.all_to_all(sectioned, "tensor", split_axis=1, concat_axis=0, tiled=True)
    wi, wb, wo = (
        lax.all_gather(
            jnp.transpose(w, (2, 1, 0)).reshape(w.shape[2], -1), "fsdp", axis=0, tiled=True
        )
        for w in regrouped
    )
    branch_in = jnp.dot(tokens, wi, preferred_element_type=jnp.float32).astype(jnp.bfloat16)
    gate_pre = jnp.dot(tokens, wb, preferred_element_type=jnp.float32)
    gated, wi, wb, gates = recur(branch_in, gate_pre, gates, rate, wi, wb, prompts)
    partial_value = lax.dot_general(gated, wo, NT, preferred_element_type=jnp.float32)
    mixed = lax.psum_scatter(
        partial_value.astype(jnp.bfloat16), "tensor", scatter_dimension=1, tiled=True
    )
    return mixed, wi, wb, wo, gates


def solution(mesh):
    return jax.shard_map(
        on_device,
        mesh=mesh,
        in_specs=(
            P("fsdp", None),
            P("tensor", None, "fsdp"),
            P("tensor", None, "fsdp"),
            P("tensor", None, "fsdp"),
            P(None, None, "fsdp", "tensor"),
            P(),
            P(),
        ),
        out_specs=(
            P("fsdp", "tensor"),
            P(None, "tensor"),
            P(None, "tensor"),
            P(None, "tensor"),
            P(None, "tensor", None, None),
        ),
        check_vma=False,
    )
```

```python
import functools
import jax
import jax.numpy as jnp
from jax import lax
from jax.experimental import pallas as pl
from jax.experimental.pallas import tpu as pltpu
from jax.sharding import PartitionSpec as P

LEN = 256
SUB = 8
VMEM_LIMIT = 60 * 2**20
MESH = pl.DeviceIdType.MESH
NT = (((1,), (1,)), ((), ()))


def recur_body(
    prompts, x_ref, pre_ref, g_ref, r_ref, wi_ref, wb_ref,
    o_ref, wi_out, wb_out, g_out, a_s, d_s, carry,
):
    @pl.when(pl.program_id(1) == 0)
    def _():
        carry[...] = jnp.zeros_like(carry)
        g_out[...] = g_ref[...]

    wi_out[...] = wi_ref[...]
    wb_out[...] = wb_ref[...]
    x = x_ref[...]
    pre_r = lax.dot_general(x, g_ref[0, 0], NT, preferred_element_type=jnp.float32)
    pre_i = lax.dot_general(x, g_ref[1, 0], NT, preferred_element_type=jnp.float32)
    a = jnp.exp(r_ref[0] * jax.nn.sigmoid(pre_r))
    a_s[...] = a
    d_s[...] = jnp.sqrt(jnp.maximum(1.0 - a * a, 0.0)) * (
        jax.nn.sigmoid(pre_i) * x.astype(jnp.float32)
    )
    rows, chan = a_s.shape
    group = lax.broadcasted_iota(jnp.int32, (SUB, chan), 0) // prompts

    def last(v):
        res = v
        for g in range(SUB // prompts - 1):
            res = jnp.where(group == g, pltpu.roll(v, (g + 1) * prompts, 0), res)
        return res

    def step(i, c):
        at = pl.ds(pl.multiple_of(i * SUB, SUB), SUB)
        a = a_s[at, :]
        d = d_s[at, :]
        shift = 1
        while shift < SUB // prompts:
            a_sh = pltpu.roll(a, shift * prompts, 0)
            d_sh = pltpu.roll(d, shift * prompts, 0)
            d = jnp.where(group >= shift, a * d_sh + d, d)
            a = jnp.where(group >= shift, a * a_sh, a)
            shift *= 2
        d_s[at, :] = a * c + d
        return last(a) * c + last(d)

    carry[...] = lax.fori_loop(0, rows // SUB, step, carry[...], unroll=8)
    o_ref[...] = (d_s[...] * jax.nn.gelu(pre_ref[...], approximate=True)).astype(o_ref.dtype)


def recur(branch_in, gate_pre, gates, rate, wi, wb, prompts):
    rows, width = branch_in.shape
    blocks, chan = gates.shape[1], gates.shape[2]
    tile = min(rows, 256)
    tiles = rows // tile
    part = wi.shape[0] // (blocks * tiles)
    cell = pl.BlockSpec((tile, chan), lambda b, t: (t, b))
    gate = pl.BlockSpec((2, 1, chan, chan), lambda b, t: (0, b, 0, 0))
    slab = pl.BlockSpec((part, width), lambda b, t: (b * tiles + t, 0))
    return pl.pallas_call(
        functools.partial(recur_body, prompts),
        grid=(blocks, tiles),
        in_specs=[cell, cell, gate, pl.BlockSpec((1, 1, chan), lambda b, t: (b, 0, 0)), slab, slab],
        out_specs=[cell, slab, slab, gate],
        out_shape=[
            jax.ShapeDtypeStruct((rows, width), jnp.bfloat16),
            jax.ShapeDtypeStruct(wi.shape, wi.dtype),
            jax.ShapeDtypeStruct(wb.shape, wb.dtype),
            jax.ShapeDtypeStruct(gates.shape, gates.dtype),
        ],
        scratch_shapes=[
            pltpu.VMEM((tile, chan), jnp.float32),
            pltpu.VMEM((tile, chan), jnp.float32),
            pltpu.VMEM((SUB, chan), jnp.float32),
        ],
        compiler_params=pltpu.CompilerParams(
            dimension_semantics=("arbitrary", "arbitrary"), vmem_limit_bytes=VMEM_LIMIT
        ),
        cost_estimate=pl.CostEstimate(
            flops=4 * rows * width * chan, bytes_accessed=8 * rows * width, transcendentals=6 * rows * width
        ),
        name="recur",
    )(branch_in, gate_pre, gates, rate, wi, wb)


def places():
    f = lax.axis_index("fsdp")
    sib = f + 1 - 2 * (f % 2)
    xp = f + 2 - 4 * ((f // 2) % 2)
    yp = f + 4 - 8 * (f // 4)
    diag = xp + 4 - 8 * (xp // 4)
    return f, sib, xp, yp, diag


def greet(zs, z, peers):
    barrier = pltpu.get_barrier_semaphore()
    for peer in peers:
        pl.semaphore_signal(barrier, inc=1, device_id={"fsdp": peer}, device_id_type=MESH)
    for k in range(1, zs):
        pl.semaphore_signal(
            barrier, inc=1, device_id={"tensor": (z + k) % zs}, device_id_type=MESH
        )


def met(zs, peers):
    pl.semaphore_wait(pltpu.get_barrier_semaphore(), len(peers) + zs - 1)


def gatherer(view, f_send, f_recv):
    f, sib, xp, yp, diag = places()

    def make(q, i):
        near, far = ((xp, yp), (yp, xp))[q % 2]
        owner, peer = (
            (f, xp), (f, yp), (f, sib), (near, far), (xp, sib), (yp, sib), (diag, sib),
        )[i]
        at = view(q, owner)
        return pltpu.make_async_remote_copy(
            src_ref=at,
            dst_ref=at,
            send_sem=f_send.at[q, i],
            recv_sem=f_recv.at[q, i],
            device_id={"fsdp": peer},
            device_id_type=MESH,
        )

    def first(q):
        for i in range(3):
            make(q, i).start()

    def relay(q):
        make(q, 0).wait_recv()
        if q % 2 == 0:
            make(q, 3).start()
        make(q, 4).start()
        make(q, 1).wait_recv()
        if q % 2 == 1:
            make(q, 3).start()
        make(q, 5).start()

    def across(q):
        make(q, 3).wait_recv()
        make(q, 6).start()

    def have(q, *ways):
        for i in ways:
            make(q, i).wait_recv()

    def hand(q):
        for i in (3, 4, 5):
            make(q, i).start()

    def drain(qs, ways=range(7)):
        for q in qs:
            for i in ways:
                make(q, i).wait_send()

    return first, relay, across, have, drain, hand


def spread_body(
    order, src0, src1, src2, gsrc, tokens,
    out0, out1, piece2, gates_out, x_out, pre_out,
    perm, srcv, xb, sbuf, gsend, held, gheld, gfull, wfull, tok, acc, acc_pre, x_held, piece_v,
    src_sem, x_sem, pre_sem, piece_sem, tok_sem, own_sem, z_send, z_recv, put_sem, f_send, f_recv,
):
    srcs = (src0, src1, src2)
    z = lax.axis_index("tensor")
    f, sib, xp, yp, diag = places()
    zs, per, chan = held.shape[2], held.shape[3], held.shape[4]
    rows = src0.shape[2]
    half = rows // 2
    ghalf = gheld.shape[3] // 2
    group = per * chan
    tok_copy = pltpu.make_async_copy(tokens, tok, tok_sem)
    src_copy = [pltpu.make_async_copy(srcs[w], srcv.at[w], src_sem.at[w]) for w in range(3)]
    src_copy[0].start()
    greet(zs, z, (sib, xp, yp))

    def cast(w):
        src_copy[w].wait()
        xb[...] = srcv[w].reshape(xb.shape).astype(jnp.bfloat16)
        for k in range(zs):
            part = jnp.dot(
                perm[k * group : (k + 1) * group, :], xb[...], preferred_element_type=jnp.float32
            )
            part = part.astype(jnp.bfloat16).reshape(per, chan, rows)
            for p in range(2):
                sbuf[w, p, k * per : (k + 1) * per] = part[:, :, p * half : (p + 1) * half]

    blocks = sbuf.shape[2]
    column = lax.broadcasted_iota(jnp.int32, (chan, perm.shape[1]), 1)
    channel = lax.broadcasted_iota(jnp.int32, (chan, perm.shape[1]), 0) * blocks
    for j in range(blocks):
        perm[j * chan : (j + 1) * chan, :] = jnp.where(
            column == channel + order[j], 1.0, 0.0
        ).astype(jnp.bfloat16)
    cast(0)
    src_copy[1].start()
    src_copy[2].start()
    tok_copy.start()
    met(zs, (sib, xp, yp))

    def z_source(q, to):
        if q == 6:
            return gsend.at[:, pl.ds(to * per, per)]
        return sbuf.at[q // 2, q % 2, pl.ds(to * per, per)]

    def z_target(q):
        if q == 6:
            return gheld.at[z]
        return held.at[q // 2, q % 2, z]

    a2a, own = {}, {}
    queue = [0, 1, 2, 6, 3, 4, 5]

    def exchange(q, i, to, sender):
        return pltpu.make_async_remote_copy(
            src_ref=z_source(q, to),
            dst_ref=z_target(q),
            send_sem=z_send.at[q, i],
            recv_sem=z_recv.at[q, sender],
            device_id={"tensor": to},
            device_id_type=MESH,
        )

    def depart():
        q = queue.pop(0)
        for i in range(zs - 1):
            up = (z + i + 1) % zs
            down = zs - 1 - (zs - z + i) % zs
            to = jnp.where(z < zs // 2, up, down)
            a2a[q, i] = exchange(q, i, to, z)
            a2a[q, i].start()
        own[q] = pltpu.make_async_copy(z_source(q, z), z_target(q), own_sem.at[q])
        own[q].start()

    depart()
    cast(1)
    cast(2)
    for g in range(gsend.shape[0]):
        for j in range(gsend.shape[1]):
            gsend[g, j] = gsrc[g, order[j]].astype(jnp.bfloat16)

    def arrive(q):
        own[q].wait()
        for k in range(1, zs):
            other = (z + k) % zs
            exchange(q, 0, other, other).wait_recv()
        for _ in range(2 if q == 0 else 1):
            if queue:
                depart()

    def slab(q, b):
        return jnp.concatenate([held[q // 2, q % 2, s, b] for s in range(zs)], axis=0).T

    def view(q, owner):
        if q >= 4:
            return gfull.at[:, :, pl.ds(owner * 2 * ghalf + (q - 4) * ghalf, ghalf)]
        return wfull.at[q // 2, pl.ds(owner * rows + (q % 2) * half, half)]

    send_first, relay, across, have, drain, _ = gatherer(view, f_send, f_recv)

    def first(q):
        if q < 4:
            arrive(q)
            at = pl.ds(pl.multiple_of(f * rows + (q % 2) * half, half), half)
            for b in range(per):
                width = chan * zs
                wfull[q // 2, at, b * width : (b + 1) * width] = slab(q, b)
        send_first(q)

    def first_out(q):
        arrive(q)
        at = slice((q % 2) * half, (q % 2) * half + half)
        for b in range(per):
            width = chan * zs
            piece_v[at, b * width : (b + 1) * width] = slab(q, b)
        piece_copy(q).start()

    def piece_copy(q):
        at = pl.ds((q % 2) * half, half)
        return pltpu.make_async_copy(piece_v.at[at], piece2.at[at], piece_sem.at[q % 2])

    put = []
    tile = 256
    deep = 2 * rows
    tiles = tok.shape[0] // tile

    def result(w, i):
        at = pl.ds(pl.multiple_of(i * tile, tile), tile)
        if w == 0:
            return pltpu.make_async_copy(x_held.at[at], x_out.at[at], x_sem.at[i])
        return pltpu.make_async_copy(acc_pre.at[at], pre_out.at[at], pre_sem.at[i])

    def product(w, part, mode):
        base = pl.multiple_of(part * deep, deep)
        outs = (out0, out1)
        copy = pltpu.make_async_copy(
            wfull.at[w, pl.ds(base, deep)], outs[w].at[pl.ds(base, deep)], put_sem.at[len(put)]
        )
        copy.start()
        put.append(copy)
        dst = (acc, acc_pre)[w]

        def step(i, c):
            at = pl.ds(pl.multiple_of(i * tile, tile), tile)
            value = jnp.dot(
                tok[at, pl.ds(base, deep)],
                wfull[w, pl.ds(base, deep), :],
                preferred_element_type=jnp.float32,
            )
            if mode != "first":
                value = value + dst[at, :]
            if w == 0 and mode == "last":
                x_held[at, :] = value.astype(jnp.bfloat16)
            else:
                dst[at, :] = value
            if mode == "last":
                result(w, i).start()
            return c

        lax.fori_loop(0, tiles, step, 0)

    chip, chip_x, chip_y, chip_d = f // 2, xp // 2, yp // 2, diag // 2

    first(0)
    first(1)
    relay(0)
    first(2)
    arrive(6)
    for h in range(2):
        for g in range(gfull.shape[0]):
            for b in range(per):
                at = pl.ds(pl.multiple_of((f * 2 + h) * ghalf, ghalf), ghalf)
                gfull[g, b, at, :] = jnp.concatenate(
                    [gheld[s, g, b, h * ghalf : (h + 1) * ghalf, :] for s in range(zs)], axis=1
                )
    first(4)
    first(5)
    relay(1)
    first(3)
    tok_copy.wait()
    have(0, 2)
    have(1, 2)
    product(0, chip, "first")
    across(0)
    relay(2)
    have(0, 4)
    have(1, 4)
    product(0, chip_x, "more")
    relay(4)
    relay(5)
    first_out(4)
    across(1)
    have(0, 5)
    have(1, 5)
    product(0, chip_y, "more")
    relay(3)
    have(0, 6)
    have(1, 6)
    product(0, chip_d, "last")
    first_out(5)
    for q in (4, 5, 2):
        across(q)
    have(2, 2)
    have(3, 2)
    product(1, chip, "first")
    have(2, 4)
    have(3, 4)
    product(1, chip_x, "more")
    across(3)
    have(2, 5)
    have(3, 5)
    product(1, chip_y, "more")
    for q in (4, 5):
        have(q, 2, 4, 5, 6)
    for g in range(gfull.shape[0]):
        for b in range(per):
            gates_out[g, b] = gfull[g, b].T
    have(2, 6)
    have(3, 6)
    product(1, chip_d, "last")
    for copy in put:
        copy.wait()
    for i in range(tiles):
        result(0, i).wait()
        result(1, i).wait()
    piece_copy(4).wait()
    piece_copy(5).wait()
    drain(range(6))
    for q in range(7):
        for i in range(zs - 1):
            a2a[q, i].wait_send()


def spread(order, sources, gates, tokens, zs, fs):
    chan, blocks, rows = sources[0].shape
    kinds, _, gin, gout = gates.shape
    per = blocks // zs
    width = per * chan * zs
    toks = tokens.shape[0]
    full = jax.ShapeDtypeStruct((rows * fs, width), jnp.bfloat16)
    vmem = pl.BlockSpec(memory_space=pltpu.VMEM)
    hbm = pl.BlockSpec(memory_space=pl.ANY)
    dma = pltpu.SemaphoreType.DMA
    return pl.pallas_call(
        spread_body,
        in_specs=[pl.BlockSpec(memory_space=pltpu.SMEM)] + [hbm] * 3 + [vmem, hbm],
        out_specs=[hbm, hbm, hbm, vmem, hbm, hbm],
        out_shape=[
            full,
            full,
            jax.ShapeDtypeStruct((rows, width), jnp.bfloat16),
            jax.ShapeDtypeStruct((kinds, per, gout * zs, gin * fs), jnp.bfloat16),
            jax.ShapeDtypeStruct((toks, width), jnp.bfloat16),
            jax.ShapeDtypeStruct((toks, width), jnp.float32),
        ],
        scratch_shapes=[
            pltpu.VMEM((chan * blocks, chan * blocks), jnp.bfloat16),
            pltpu.VMEM((3, chan, blocks, rows), jnp.float32),
            pltpu.VMEM((chan * blocks, rows), jnp.bfloat16),
            pltpu.VMEM((3, 2, blocks, chan, rows // 2), jnp.bfloat16),
            pltpu.VMEM((kinds, blocks, gin, gout), jnp.bfloat16),
            pltpu.VMEM((3, 2, zs, per, chan, rows // 2), jnp.bfloat16),
            pltpu.VMEM((zs, kinds, per, gin, gout), jnp.bfloat16),
            pltpu.VMEM((kinds, per, gin * fs, gout * zs), jnp.bfloat16),
            pltpu.VMEM((2, rows * fs, width), jnp.bfloat16),
            pltpu.VMEM(tokens.shape, jnp.bfloat16),
            pltpu.VMEM((toks, width), jnp.float32),
            pltpu.VMEM((toks, width), jnp.float32),
            pltpu.VMEM((toks, width), jnp.bfloat16),
            pltpu.VMEM((rows, width), jnp.bfloat16),
            dma((3,)),
            dma((toks // 256,)),
            dma((toks // 256,)),
            dma((2,)),
            dma,
            dma((7,)),
            dma((7, zs)),
            dma((7, zs)),
            dma((8,)),
            dma((6, 7)),
            dma((6, 7)),
        ],
        compiler_params=pltpu.CompilerParams(
            collective_id=0, has_side_effects=True, vmem_limit_bytes=VMEM_LIMIT
        ),
        name="spread",
    )(order, *sources, gates, tokens)


def chain_body(
    gated, piece, piece_x, piece_y, piece_s, extra, out, mixed,
    wfull, wend, rows_in, early_out, early_right, early_left, late_out, late_right, late_left,
    put_sem, get_sem, r_send, r_recv, l_send, l_recv, f_send, f_recv,
):
    z = lax.axis_index("tensor")
    zs = lax.axis_size("tensor")
    f, sib, xp, yp, diag = places()
    rows = piece.shape[0]
    parts = 4
    part = rows // parts
    cut, rt = early_out.shape[2], early_out.shape[1]
    wide, lt = late_out.shape[3], late_out.shape[2]
    cuts = wfull.shape[0] // cut
    quarter = cuts // zs
    halves = rows // cut
    late = (gated.shape[0] - rt) // lt
    pair = 2
    inner = (z > 0) & (z < zs - 1)
    greet(zs, z, (sib, xp, yp))
    gets = []
    for ref, to, owner in (
        (piece_x, wfull, xp), (piece_y, wfull, yp), (piece, wfull, f), (piece_s, wfull, sib), (extra, wend, f),
    ):
        at = pl.ds(pl.multiple_of(owner * rows, rows), rows)
        gets.append(pltpu.make_async_copy(ref, to.at[at], get_sem.at[len(gets)]))
        gets[-1].start()
    met(zs, (sib, xp, yp))

    def view(q, owner):
        to = wfull if q < parts else wend
        return to.at[pl.ds(owner * rows + (q % parts) * part, part)]

    first, relay, across, have, drain, hand = gatherer(view, f_send, f_recv)

    def dot(x, w, at):
        return lax.dot_general(x, w[at, :], NT, preferred_element_type=jnp.float32)

    def early_term(d):
        return dot(gated[:rt, :], wfull, pl.ds(d * cut, cut))

    def late_rows(t):
        return slice(rt + t * lt, rt + (t + 1) * lt)

    def late_term(t, q):
        return dot(gated[late_rows(t), :], wfull, pl.ds(q * wide, wide))

    def end_term(t, q):
        return dot(rows_in[t * lt : (t + 1) * lt, :], wend, pl.ds(q * wide, wide))

    def move(src, dst, s, forward):
        return pltpu.make_async_remote_copy(
            src_ref=src,
            dst_ref=dst,
            send_sem=(r_send if forward else l_send).at[s],
            recv_sem=(r_recv if forward else l_recv).at[s],
            device_id={"tensor": (z + (1 if forward else zs - 1)) % zs},
            device_id_type=MESH,
        )

    def early_move(d, forward):
        ins = early_right if forward else early_left
        return move(early_out.at[d], ins.at[d], d, forward)

    def late_move(t, q, forward):
        ins = late_right if forward else late_left
        return move(late_out.at[q, t], ins.at[q, t], cuts + q * late + t, forward)

    def row_move(t, forward):
        return move(
            gated.at[pl.ds(rt + t * lt // pair, lt // pair)], rows_in.at[pl.ds(t * lt // pair, lt // pair)],
            cuts + zs * late + t, forward,
        )

    def ordered(q):
        return sorted(range(q * quarter, (q + 1) * quarter), key=lambda d: (d % halves, d))

    lists, sends = {}, {}
    for forward in (True, False):
        far = range(zs - 1, 0, -1) if forward else range(zs - 1)
        groups = [[("early", d) for d in ordered(q)] for q in far]
        lists[forward] = [item for group in groups for item in group]
        at = (zs - 2) * quarter
        lists[forward][at:at] = [("rows", t) for t in range(pair, pair * late)]
        lists[forward][at - 1 : at - 1] = [("rows", t) for t in range(pair)]
        sends[forward] = list(lists[forward])
        sends[forward].insert(0, sends[forward].pop(at - 1))

    def one(forward, k):
        kind, n = sends[forward][k]
        return early_move(n, forward) if kind == "early" else row_move(n, forward)

    def early_pass(d, forward):
        value = early_term(d)
        early_move(d, forward).wait_recv()
        ins = early_right if forward else early_left
        early_out[d] = (value + ins[d].astype(jnp.float32)).astype(jnp.bfloat16)
        early_move(d, forward).start()

    def late_pass(t, q, forward):
        value = late_term(t, q)
        late_move(t, q, forward).wait_recv()
        ins = late_right if forward else late_left
        late_out[q, t] = (value + ins[q, t].astype(jnp.float32)).astype(jnp.bfloat16)
        late_move(t, q, forward).start()

    def end(forward, away):
        return z == (away if forward else zs - 1 - away)

    def beyond(forward, away):
        return range(zs - 1, away, -1) if forward else range(zs - 1 - away)

    def step(k):
        for forward in (True, False):
            if k + 1 < len(sends[forward]):
                given, m = sends[forward][k + 1]

                @pl.when(end(forward, 0))
                def _():
                    if given == "early":
                        early_out[m] = early_term(m).astype(jnp.bfloat16)
                    if k >= 1:
                        one(forward, k - 1).wait_send()
                    one(forward, k + 1).start()

            kind, n = lists[forward][k]
            if kind == "rows":
                @pl.when(end(forward, 1))
                def _():
                    if n % pair < pair - 1:
                        row_move(n, forward).wait_recv()
                        return
                    t = n // pair
                    values = [late_term(t, q) for q in beyond(forward, 1)]
                    row_move(n, forward).wait_recv()
                    for q, value in zip(beyond(forward, 1), values):
                        late_out[q, t] = (value + end_term(t, q)).astype(jnp.bfloat16)
                        late_move(t, q, forward).start()

        for forward in (True, False):
            kind, n = lists[forward][k]
            for away in range(1, zs - 1):
                if kind == "early":
                    if n // quarter in beyond(forward, away):
                        @pl.when(end(forward, away))
                        def _():
                            early_pass(n, forward)
                elif away > 1 and n % pair == pair - 1:
                    @pl.when(end(forward, away))
                    def _():
                        for q in beyond(forward, away):
                            late_pass(n // pair, q, forward)

    def all_of(q):
        have(q, 2, 4, 5, 6)

    def when_inner(*acts):
        @pl.when(inner)
        def _():
            for act, q in acts:
                act(q)

    def last_late(c, t):
        value = late_term(t, c)
        if c in (1, zs - 2):
            value = value + end_term(t, c)
        if c > 1:
            late_move(t, c, True).wait_recv()
            value = value + late_right[c, t].astype(jnp.float32)
        if c < zs - 2:
            late_move(t, c, False).wait_recv()
            value = value + late_left[c, t].astype(jnp.float32)
        mixed[late_rows(t), :] = value.astype(mixed.dtype)

    def last_early(c, d):
        value = early_term(d)
        if c < zs - 1:
            early_move(d, False).wait_recv()
            value = value + early_left[d].astype(jnp.float32)
        if c > 0:
            early_move(d, True).wait_recv()
            value = value + early_right[d].astype(jnp.float32)
        e = d - c * quarter
        mixed[:rt, e * cut : (e + 1) * cut] = value.astype(mixed.dtype)

    def on_each(cs, act):
        for c in cs:
            @pl.when(z == c)
            def _():
                act(c)

    for forward in (True, False):
        @pl.when(end(forward, 0))
        def _():
            one(forward, 0).start()

    for get in gets[:2]:
        get.wait()
    hand(0)
    hand(1)
    for get in gets[2:]:
        get.wait()
    across(0)
    across(1)
    hand(2)
    hand(3)
    when_inner((first, parts), (first, parts + 1))
    have(0, 4, 5, 6)
    have(1, 4, 5, 6)
    step(0)
    across(2)
    across(3)
    step(1)
    have(2, 4, 5, 6)
    have(3, 4, 5, 6)
    put = pltpu.make_async_copy(wfull, out, put_sem)
    put.start()
    when_inner((relay, parts), (relay, parts + 1), (first, parts + 2), (first, parts + 3))
    step(2)
    step(3)
    when_inner((across, parts), (across, parts + 1))
    step(4)
    when_inner((relay, parts + 2), (relay, parts + 3))
    step(5)
    step(6)
    when_inner((across, parts + 2), (across, parts + 3))
    step(7)
    when_inner(*((all_of, parts + q) for q in range(parts)))
    count = len(lists[True])
    ends = (0, zs - 1)
    for k in range(8, count):
        step(k)
        if k < 8 + quarter:
            on_each(ends, lambda c: last_early(c, ordered(c)[k - 8]))
        if (count - 1 - k) % 2 == 0 and k > count - 1 - 2 * late:
            on_each(range(zs), lambda c: last_late(c, late - 1 - (count - 1 - k) // 2))

    for c in range(zs):
        @pl.when(z == c)
        def _():
            if c not in ends:
                for d in ordered(c):
                    last_early(c, d)
            for forward in (True, False):
                away = c if forward else zs - 1 - c
                if away == 0:
                    for k in range(count - 2, count):
                        one(forward, k).wait_send()
                else:
                    for q in beyond(forward, away):
                        for d in ordered(q):
                            early_move(d, forward).wait_send()
                        for t in range(late):
                            late_move(t, q, forward).wait_send()

    drain(range(parts), range(3, 7))
    when_inner((drain, range(parts, 2 * parts)))
    put.wait()


def chain(gated, piece, near, extra, zs, fs):
    rows, width = piece.shape
    toks = gated.shape[0]
    depth = rows * fs
    cut, rt = rows // 2, toks // 2
    wide, lt = depth // zs, toks // 4
    late = (toks - rt) // lt
    vmem = pl.BlockSpec(memory_space=pltpu.VMEM)
    hbm = pl.BlockSpec(memory_space=pl.ANY)
    dma = pltpu.SemaphoreType.DMA
    early_buf = pltpu.VMEM((depth // cut, rt, cut), jnp.bfloat16)
    late_buf = pltpu.VMEM((zs, late, lt, wide), jnp.bfloat16)
    sems = dma((depth // cut + (zs + 2) * late,))
    return pl.pallas_call(
        chain_body,
        in_specs=[vmem] + [hbm] * 5,
        out_specs=[hbm, vmem],
        out_shape=[
            jax.ShapeDtypeStruct((depth, width), jnp.bfloat16),
            jax.ShapeDtypeStruct((toks, depth // zs), jnp.bfloat16),
        ],
        scratch_shapes=[
            pltpu.VMEM((depth, width), jnp.bfloat16),
            pltpu.VMEM((depth, width), jnp.bfloat16),
            pltpu.VMEM((toks - rt, width), jnp.bfloat16),
            early_buf,
            early_buf,
            early_buf,
            late_buf,
            late_buf,
            late_buf,
            dma,
            dma((5,)),
            sems,
            sems,
            sems,
            sems,
            dma((8, 7)),
            dma((8, 7)),
        ],
        compiler_params=pltpu.CompilerParams(
            collective_id=1, has_side_effects=True, vmem_limit_bytes=VMEM_LIMIT
        ),
        name="chain",
    )(gated, piece, *near, extra)


def dup_body(x_ref, y_ref, x_out, y_out):
    x_out[...] = x_ref[...]
    y_out[...] = y_ref[...]


def dup(x, y):
    steps = 8
    specs = [pl.BlockSpec((a.shape[0] // steps, a.shape[1]), lambda i: (i, 0)) for a in (x, y)]
    return pl.pallas_call(
        dup_body,
        grid=(steps,),
        in_specs=specs,
        out_specs=specs,
        out_shape=[jax.ShapeDtypeStruct(a.shape, a.dtype) for a in (x, y)],
        cost_estimate=pl.CostEstimate(flops=0, bytes_accessed=4 * (x.size + y.size), transcendentals=0),
        name="dup",
    )(x, y)


def on_device(
    tokens, input_source, branch_source, output_source, gates_source, decay_param, block_order
):
    zs, fs = lax.axis_size("tensor"), lax.axis_size("fsdp")
    blocks = block_order.shape[0]
    per_dev = blocks // zs
    prompts = tokens.shape[0] // LEN
    picked = (block_order[:, None] == jnp.arange(blocks)[None, :]).astype(jnp.float32)
    soft = -8.0 * jax.nn.softplus(decay_param)
    own = lax.dynamic_slice_in_dim(picked, lax.axis_index("tensor") * per_dev, per_dev)
    rate = jnp.sum(own[:, :, None] * soft[None, :, :], axis=1)[:, None, :]
    sources = (input_source, branch_source, output_source)
    if fs == 8 and zs == 4:
        wi, wb, piece, gates, branch_in, gate_pre = spread(
            block_order, sources, gates_source, tokens, zs, fs
        )
        near = [
            lax.ppermute(piece, "fsdp", [(f, peer(f)) for f in range(fs)])
            for peer in (
                lambda f: f + 2 - 4 * ((f // 2) % 2),
                lambda f: f + 4 - 8 * (f // 4),
                lambda f: f + 1 - 2 * (f % 2),
            )
        ]
        extra = lax.ppermute(piece, "tensor", [(0, 1), (zs - 1, zs - 2)])
        gated, wi, wb, gates = recur(branch_in, gate_pre, gates, rate, wi, wb, prompts)
        wo, mixed = chain(gated, piece, near, extra, zs, fs)
        wo, mixed = dup(wo, mixed)
        return mixed, wi, wb, wo, gates
    hot = picked.astype(jnp.bfloat16)
    sectioned = tuple(
        jnp.einsum(
            "jb,cbr->cjr", hot, s.astype(jnp.bfloat16), preferred_element_type=jnp.float32
        ).astype(jnp.bfloat16)
        for s in sources
    )
    gate_sectioned = jnp.einsum(
        "jb,gbio->gjio", hot, gates_source.astype(jnp.bfloat16), preferred_element_type=jnp.float32
    ).astype(jnp.bfloat16)
    gate_group = lax.all_to_all(gate_sectioned, "tensor", split_axis=1, concat_axis=3, tiled=True)
    gates = lax.all_gather(jnp.transpose(gate_group, (0, 1, 3, 2)), "fsdp", axis=3, tiled=True)
    regrouped = lax.all_to_all(sectioned, "tensor", split_axis=1, concat_axis=0, tiled=True)
    wi, wb, wo = (
        lax.all_gather(
            jnp.transpose(w, (2, 1, 0)).reshape(w.shape[2], -1), "fsdp", axis=0, tiled=True
        )
        for w in regrouped
    )
    branch_in = jnp.dot(tokens, wi, preferred_element_type=jnp.float32).astype(jnp.bfloat16)
    gate_pre = jnp.dot(tokens, wb, preferred_element_type=jnp.float32)
    gated, wi, wb, gates = recur(branch_in, gate_pre, gates, rate, wi, wb, prompts)
    partial_value = lax.dot_general(gated, wo, NT, preferred_element_type=jnp.float32)
    mixed = lax.psum_scatter(
        partial_value.astype(jnp.bfloat16), "tensor", scatter_dimension=1, tiled=True
    )
    return mixed, wi, wb, wo, gates


def solution(mesh):
    return jax.shard_map(
        on_device,
        mesh=mesh,
        in_specs=(
            P("fsdp", None),
            P("tensor", None, "fsdp"),
            P("tensor", None, "fsdp"),
            P("tensor", None, "fsdp"),
            P(None, None, "fsdp", "tensor"),
            P(),
            P(),
        ),
        out_specs=(
            P("fsdp", "tensor"),
            P(None, "tensor"),
            P(None, "tensor"),
            P(None, "tensor"),
            P(None, "tensor", None, None),
        ),
        check_vma=False,
    )
```
